32 devices in a mesh: group: 4 (over y, core), region: 8 (over z, x).
Axes of the slice: x: 2, y: 2, z: 4, core: 2. Of those that a mesh axis runs over, the one named last changes fastest.
Arguments:
- observed: float32 [65536], P(('group', 'region')), may hold values from -6 to 6
- noise_precision: float32 [65536], P(('group', 'region')), may hold values from 0.25 to 4
- mid_basis: float32 [65536, 512], P(('group', 'region')), may hold values from -0.077339804 to 0.077339804
- root_basis: float32 [65536, 512], P(('group', 'region')), may hold values from -0.038669902 to 0.038669902
- mid_prior: float32 [4, 512], P('group'), may hold values from 0.3 to 3
- root_prior: float32 [512], replicated, may hold values from 0.3 to 3
- leaf_count: int32 [4, 8], P('group', 'region'), may hold values from 1024 to 2048, as said below
Outputs:
- root_weight_means: float32 [512], replicated
- middle_weight_means: float32 [4, 512], P('group', 'region')
- leaf_fit: float32 [65536], P(('group', 'region'))
The draws below stay inside these ranges and needn't reach their ends.
Inputs may be any that keep to these rules, and one draw needn't show every extreme that they name: `leaf_count`: every entry lies between 1024 and 2048, and some region has all 2048 slots live.
All inputs are finite; a program needn't handle non-finite values.
Results may differ from the reference program's by a relative error of at most 0.0012.
Values sent between devices are 32-bit elements; how exact they have to be, the bound alone decides.
A program may use at most 64 MiB of HBM per device.

```python
import math
import jax
import jax.numpy as jnp
from jax import lax

L = 2048
M = 512
R = 512
GROUPS = 4
REGIONS = 8
GROUP_OBS = 16384
OBS = 65536
N_GROUP = 4
N_REGION = 8


energy_level = 8.0


clip_level = 3.5


shared_part = 0.8


fresh_part = 0.6


mid_stretch_divisor = 1.5


root_stretch_divisor = 6.0


def draw_leaf_count(key, part):
    counts = jax.random.randint(key, (GROUPS * REGIONS,), L // 2, L + 1)
    chosen = jax.random.randint(jax.random.fold_in(key, 7), (), 0, GROUPS * REGIONS)
    counts = jnp.where(jnp.arange(GROUPS * REGIONS) == chosen, L, counts)
    return counts.reshape(GROUPS, REGIONS).astype(jnp.int32)


def knot_mixing(base_key, knot_count, divisor):
    points = jax.random.uniform(base_key, (knot_count, 2), jnp.float32)
    offsets = points[:, None, :] - points[None, :, :]
    distance = jnp.sqrt(jnp.sum(offsets * offsets, axis=-1))
    stretch = math.sqrt(knot_count) / divisor
    scaled = distance * stretch
    kernel = (1.0 + scaled) * jnp.exp(-scaled)
    return kernel / jnp.sqrt(jnp.sum(kernel * kernel, axis=0, keepdims=True))


def latent_block(row_key, width):
    return jax.random.normal(row_key, (GROUP_OBS, width), jnp.float32)


def shared_latent(key, group_index):
    return latent_block(jax.random.fold_in(jax.random.fold_in(key, 41), group_index), max(M, R))


def basis_rows(latent, mixing, spread):
    rows = jnp.dot(latent, mixing, precision=lax.Precision.HIGHEST, preferred_element_type=jnp.float32) * spread
    limit = clip_level * spread
    return jnp.clip(rows, -limit, limit)


def draw_mid_basis(key, part):
    base_key = jax.random.fold_in(key, 11)
    spread = math.sqrt(energy_level / GROUP_OBS)

    def one_group(group_index):
        mixing = knot_mixing(jax.random.fold_in(base_key, 2 * group_index + 1), M, mid_stretch_divisor)
        latent = shared_latent(key, group_index)[:, :M]
        return basis_rows(latent, mixing, spread)
    return lax.map(one_group, jnp.arange(GROUPS, dtype=jnp.int32)).reshape(OBS, M)


def draw_root_basis(key, part):
    base_key = jax.random.fold_in(key, 23)
    mixing = knot_mixing(jax.random.fold_in(key, 29), R, root_stretch_divisor)
    spread = math.sqrt(energy_level / OBS)

    def one_group(group_index):
        fresh = latent_block(jax.random.fold_in(base_key, group_index), R)
        latent = shared_part * shared_latent(key, group_index)[:, :R] + fresh_part * fresh
        return basis_rows(latent, mixing, spread)
    return lax.map(one_group, jnp.arange(GROUPS, dtype=jnp.int32)).reshape(OBS, R)


def levels(stream_key, dims, pieces, smallest, top_value):
    gain, own = 1.0, jax.random.fold_in(stream_key, 6)
    for position, blocks in pieces:
        draws = jnp.exp(jax.random.uniform(jax.random.fold_in(own, position), (blocks,), jnp.float32, smallest / len(pieces), top_value / len(pieces)))
        gain = gain * jnp.repeat(draws, dims[position] // blocks).reshape([-1 if axis == position else 1 for axis in range(len(dims))])
    return gain


def centred(key, dims, scale, most, shards=(), held_as=jnp.bfloat16):
    entries = scale * jax.random.normal(key, dims, jnp.float32)
    if shards:
        entries = entries * levels(key, dims, shards, -0.22, 0.18)
    return jnp.clip(entries, -most, most).astype(held_as)


def setup_inputs(seed: int = 0) -> dict:
    splits = jax.random.split(jax.random.key(seed), 8)
    return {
        "observed": centred(splits[0], (OBS,), 1.0, 6.0, ((0, 32),), jnp.float32),
        "noise_precision": jnp.clip(jnp.exp(math.log(4.0) - 2.7725887 * jax.random.uniform(splits[1], (OBS,), jnp.float32) ** levels(splits[1], (OBS,), ((0, 32),), -0.2, 0.2)), 0.25, 4.0),
        "mid_basis": draw_mid_basis(jax.random.fold_in(splits[7], 71), 0),
        "root_basis": draw_root_basis(jax.random.fold_in(splits[7], 71), 0),
        "mid_prior": jnp.clip(jnp.exp(math.log(3.0) - 2.3025851 * jax.random.uniform(splits[4], (GROUPS, M), jnp.float32) ** levels(splits[4], (GROUPS, M), ((0, 4),), -0.2, 0.2)), 0.3, 3.0),
        "root_prior": jnp.clip(jnp.exp(jax.random.uniform(splits[5], (R,), jnp.float32, math.log(0.3), math.log(3.0))), 0.3, 3.0),
        "leaf_count": draw_leaf_count(jax.random.fold_in(splits[7], 71), 0),
    }


highest_precision = lax.Precision.HIGHEST

def inner_gram(former, latter):
    return lax.dot_general(former.astype(jnp.float32), latter.astype(jnp.float32), (((0,), (0,)), ((), ())), precision=highest_precision, preferred_element_type=jnp.float32)

def cholesky_solve(factor, rhs):
    column = rhs.ndim == 1
    matrix = rhs[:, None] if column else rhs
    lower_solved = lax.linalg.triangular_solve(factor, matrix, left_side=True, lower=True)
    result = lax.linalg.triangular_solve(factor, lower_solved, left_side=True, lower=True, transpose_a=True)
    return result[:, 0] if column else result

def reference(observed, noise_precision, mid_basis, root_basis, mid_prior, root_prior, leaf_count):
    per_group = L * N_REGION
    live = (jnp.arange(L, dtype=jnp.int32)[None, None, :] < leaf_count[:, :, None]).astype(jnp.float32)
    weight = noise_precision.reshape(N_GROUP, per_group) * live.reshape(N_GROUP, per_group)
    values = observed.reshape(N_GROUP, per_group)
    mid_rows = mid_basis.reshape(N_GROUP, per_group, M)
    root_rows = root_basis.reshape(N_GROUP, per_group, R)

    def group_contributions(items):
        values_g, weight_g, mid_g, root_g, prior_g = items
        weighted_obs = values_g * weight_g
        weighted_mid = mid_g * weight_g[:, None]
        mid_gram = inner_gram(weighted_mid, mid_g) + jnp.diag(prior_g)
        cross = inner_gram(weighted_mid, root_g)
        mid_rhs = jnp.dot(weighted_obs.astype(jnp.float32), mid_g.astype(jnp.float32), precision=highest_precision, preferred_element_type=jnp.float32)
        root_gram = inner_gram(root_g * weight_g[:, None], root_g)
        root_rhs = jnp.dot(weighted_obs.astype(jnp.float32), root_g.astype(jnp.float32), precision=highest_precision, preferred_element_type=jnp.float32)
        factor = jnp.linalg.cholesky(mid_gram)
        solved_cross_terms = cholesky_solve(factor, cross)
        solved_right_hand = cholesky_solve(factor, mid_rhs)
        reduced_gram = root_gram - inner_gram(cross, solved_cross_terms)
        reduced_rhs = root_rhs - jnp.dot(solved_right_hand.astype(jnp.float32), cross.astype(jnp.float32), precision=highest_precision, preferred_element_type=jnp.float32)
        return (reduced_gram, reduced_rhs, solved_cross_terms, solved_right_hand)
    reduced_gram, reduced_rhs, solved_cross_terms, solved_right_hand = lax.map(group_contributions, (values, weight, mid_rows, root_rows, mid_prior))
    root_matrix = jnp.sum(reduced_gram, axis=0) + jnp.diag(root_prior)
    root_vector = jnp.sum(reduced_rhs, axis=0)
    root_factor = jnp.linalg.cholesky(root_matrix)
    root_weight_means = cholesky_solve(root_factor, root_vector)
    middle_weight_means = solved_right_hand - jnp.einsum('wok,k->wo', solved_cross_terms, root_weight_means, precision=highest_precision)
    fit_mid = jnp.einsum('gnm,gm->gn', mid_rows, middle_weight_means, precision=highest_precision).reshape(-1)
    fit_root = jnp.dot(root_basis.astype(jnp.float32), root_weight_means.astype(jnp.float32), precision=highest_precision, preferred_element_type=jnp.float32)
    return (root_weight_means, middle_weight_means, fit_mid + fit_root)
```

```python
import functools

import jax
import jax.numpy as jnp
from jax import lax
from jax.experimental import pallas as pl
from jax.experimental.pallas import tpu as pltpu
from jax.sharding import PartitionSpec as P

HIGHEST = lax.Precision.HIGHEST
MESH = pl.DeviceIdType.MESH
BLOCK = 128
PANEL = 8
WIDE = 16
LOADS = 4


def mxu(a, b):
    return jnp.dot(a, b, precision=HIGHEST, preferred_element_type=jnp.float32)


def mxu_tn(a, b):
    return lax.dot_general(
        a, b, (((0,), (0,)), ((), ())), precision=HIGHEST, preferred_element_type=jnp.float32
    )


def mxu_nt(a, b):
    return lax.dot_general(
        a, b, (((1,), (1,)), ((), ())), precision=HIGHEST, preferred_element_type=jnp.float32
    )


def split(x):
    high = x.astype(jnp.bfloat16)
    return high, (x - high.astype(jnp.float32)).astype(jnp.bfloat16)


def split3(x):
    high = x.astype(jnp.bfloat16)
    rest = x - high.astype(jnp.float32)
    mid = rest.astype(jnp.bfloat16)
    return high, mid, (rest - mid.astype(jnp.float32)).astype(jnp.bfloat16)


def bf(a, b):
    return jnp.dot(a, b, preferred_element_type=jnp.float32)


def beside(a, b):
    return jnp.concatenate([a, b], axis=1)


def above(a, b):
    return jnp.concatenate([a, b], axis=0)


def negated_inverse(groups):
    count = len(groups)
    size = count * PANEL
    shape = (PANEL, size)
    per = WIDE // PANEL
    lane = lax.broadcasted_iota(jnp.int32, shape, 1)
    sub = lax.broadcasted_iota(jnp.int32, shape, 0)

    def row_of(value, k):
        return jnp.broadcast_to(value[k : k + 1, :], shape)

    def column_of(value, k):
        return jnp.broadcast_to(value[:, k : k + 1], shape)

    for p in range(size // WIDE):
        first = p * WIDE
        inside = (lane >= first) & (lane < first + WIDE)
        mine = groups[p * per : (p + 1) * per]
        cols = [[column_of(g, first + k) for g in mine] for k in range(WIDE)]
        work = [
            jnp.where(lane == first + PANEL * i + sub, -1.0, jnp.where(inside, 0.0, g))
            for i, g in enumerate(mine)
        ]
        for k in range(0, WIDE, 2):
            at, s = k // PANEL, k % PANEL
            left, right = cols[k], cols[k + 1]
            top, side, low = row_of(left[at], s), row_of(right[at], s), row_of(right[at], s + 1)
            inv = 1.0 / (top * low - side * side)
            inv_top, inv_side, inv_low = low * inv, -side * inv, top * inv
            former = [left[v] * inv_top + right[v] * inv_side for v in range(per)]
            latter = [left[v] * inv_side + right[v] * inv_low for v in range(per)]
            former[at] = jnp.where(sub == s, -inv_top, jnp.where(sub == s + 1, -inv_side, former[at]))
            latter[at] = jnp.where(sub == s, -inv_side, jnp.where(sub == s + 1, -inv_low, latter[at]))
            pivot = (sub == s) | (sub == s + 1)

            def cleared(target):
                upper, lower = row_of(target[at], s), row_of(target[at], s + 1)
                base = list(target)
                base[at] = jnp.where(pivot, 0.0, base[at])
                return [base[v] - former[v] * upper - latter[v] * lower for v in range(per)]

            for j in range(k + 2, WIDE):
                cols[j] = cleared(cols[j])
            work = cleared(work)
        near = [i for i in range((p + 1) * per, (p + 2) * per) if i < count]
        far = [i for i in range(count) if i // per != p and i not in near]
        after = list(groups)
        spread = [row_of(work[k // PANEL], k % PANEL) for k in range(WIDE)]
        for i in near:
            value = jnp.where(inside, 0.0, groups[i])
            for k in range(WIDE):
                value = value - column_of(groups[i], first + k) * spread[k]
            after[i] = value
        blank = jnp.zeros(shape, jnp.float32)
        padded = [work[i - p * per] if i // per == p else blank for i in range(count)]
        row_high, row_mid, row_low = split3(jnp.concatenate(padded, axis=0))
        high, mid, low = split3(jnp.concatenate(groups, axis=0))
        both = beside(high, mid)
        product = (
            bf(both, above(row_high, row_high))
            + bf(both, above(row_mid, row_mid))
            + bf(beside(low, high), above(row_high, row_low))
        )
        for i in far:
            after[i] = jnp.where(inside, 0.0, groups[i]) - product[i * PANEL : (i + 1) * PANEL, :]
        for i in range(per):
            after[p * per + i] = work[i]
        groups = after
    return groups


def each_block(a_ref, inv_ref, hooks, tails):
    blocks = a_ref.shape[0] // BLOCK

    def step(kb, carry):
        own = pl.ds(pl.multiple_of(kb * BLOCK, BLOCK), BLOCK)
        diagonal = a_ref[own, own]
        groups = [diagonal[i * PANEL : (i + 1) * PANEL, :] for i in range(BLOCK // PANEL)]
        inverse = -jnp.concatenate(negated_inverse(groups), axis=0)
        inv_ref[own, :] = inverse
        for at, hook in hooks.items():
            pl.when(kb == at)(hook)
        for at, tail in tails.items():
            pl.when(kb == at)(tail)
        return carry

    lax.fori_loop(0, blocks, step, 0)


def eliminate(a_ref, row_ref, inv_ref, k, first, last):
    if first >= last:
        return
    cols = slice(first * BLOCK, last * BLOCK)
    upper = a_ref[span(k), cols]
    row = mxu(inv_ref[span(k), :], upper)
    row_ref[span(k), cols] = row
    a_ref[cols, cols] = a_ref[cols, cols] - mxu_tn(upper, row)


def factor_tails(a_ref, row_ref, inv_ref, part, arrive):
    blocks = a_ref.shape[0] // BLOCK
    rest = slice(part * BLOCK, blocks * BLOCK)

    def lead_tail(k):
        eliminate(a_ref, row_ref, inv_ref, k, k + 1, part)

    def join():
        arrive()
        for k in range(part):
            upper = a_ref[span(k), rest]
            row = mxu(inv_ref[span(k), :], upper)
            row_ref[span(k), rest] = row
            if k + 1 < part:
                inner = slice((k + 1) * BLOCK, part * BLOCK)
                a_ref[inner, rest] = a_ref[inner, rest] - mxu_tn(a_ref[span(k), inner], row)
            a_ref[rest, rest] = a_ref[rest, rest] - mxu_tn(upper, row)

    def rest_tail(k):
        eliminate(a_ref, row_ref, inv_ref, k, k + 1, blocks)

    tails = {k: functools.partial(lead_tail, k) for k in range(part - 1)}
    tails[part - 1] = join
    for k in range(part, blocks - 1):
        tails[k] = functools.partial(rest_tail, k)
    return tails


def span(i):
    return slice(i * BLOCK, (i + 1) * BLOCK)


def block_pairs(first, last):
    return [(i, j) for i in range(first, last) for j in range(i + 1)]


def diagonal_of(prior_ref, i):
    rows = lax.broadcasted_iota(jnp.int32, (BLOCK, BLOCK), 0)
    cols = lax.broadcasted_iota(jnp.int32, (BLOCK, BLOCK), 1)
    return jnp.where(rows == cols, prior_ref[:, span(i)], 0.0)


def place_upper(matrix_ref, packed_ref, prior_ref, pairs):
    for t, (i, j) in enumerate(pairs):
        value = packed_ref[span(t), :]
        if i == j:
            matrix_ref[span(i), span(i)] = value + diagonal_of(prior_ref, i)
        else:
            turned = value.T
            matrix_ref[span(j), span(i)] = turned
            if symmetric_at(pairs, j):
                matrix_ref[span(i), span(j)] = value


def symmetric_at(pairs, j):
    return (j, j) in pairs


def fill(packed_ref, base, value):
    tail = packed_ref.shape[0] - base
    if tail:
        packed_ref[base:, :] = jnp.zeros((tail, BLOCK), jnp.float32)
    if value is not None:
        for i in range(value.shape[1] // BLOCK):
            packed_ref[base + i : base + i + 1, :] = value[0:1, span(i)]


def unpack_row(packed_ref, base, size):
    parts = [packed_ref[base + i : base + i + 1, :] for i in range(size // BLOCK)]
    return jnp.broadcast_to(jnp.concatenate(parts, axis=1), (PANEL, size))


class Exchange:
    def __init__(self, regions, slot, refs, sems):
        self.me = lax.axis_index("region")
        self.parity = self.me % 2
        self.place = self.me // 2
        self.line_count = regions // 2
        self.slot = slot
        self.buffer, self.total, self.pair_land, self.half_sum, self.line_land = refs
        self.pair_send, self.pair_recv, self.line_send, self.line_recv = sems
        self.half = self.buffer.shape[0] // 2
        self.slab = self.half // self.line_count

    def half_at(self, parity):
        return pl.ds(pl.multiple_of(parity * self.half, PANEL), self.half)

    def slab_at(self):
        start = self.parity * self.half + self.place * self.slab
        return pl.ds(pl.multiple_of(start, PANEL), self.slab)

    def part_at(self, place):
        return pl.ds(pl.multiple_of(place * self.slab, PANEL), self.slab)

    def pair_copy(self, which, source, target):
        return pltpu.make_async_remote_copy(
            src_ref=source,
            dst_ref=target,
            send_sem=self.pair_send.at[self.slot * 2 + which],
            recv_sem=self.pair_recv.at[self.slot * 2 + which],
            device_id={"region": self.me + 1 - 2 * self.parity},
            device_id_type=MESH,
        )

    def line_copy(self, which, d, source, target):
        place = (self.place + d) % self.line_count
        return pltpu.make_async_remote_copy(
            src_ref=source(place),
            dst_ref=target,
            send_sem=self.line_send.at[self.slot * 2 + which, d - 1],
            recv_sem=self.line_recv.at[self.slot * 2 + which, d - 1],
            device_id={"region": place * 2 + self.parity},
            device_id_type=MESH,
        )

    def first(self):
        return self.pair_copy(0, self.buffer.at[self.half_at(1 - self.parity)], self.pair_land)

    def second(self):
        return [
            self.line_copy(
                0, d, lambda place: self.half_sum.at[self.part_at(place)], self.line_land.at[d - 1]
            )
            for d in range(1, self.line_count)
        ]

    def third(self):
        own = self.slab_at()
        return [
            self.line_copy(1, d, lambda place: self.total.at[own], self.total.at[own])
            for d in range(1, self.line_count)
        ]

    def last(self):
        mine = self.total.at[self.half_at(self.parity)]
        return self.pair_copy(1, mine, mine)

    def start_pair(self):
        self.first().start()

    def start_line(self):
        self.first().wait()
        self.half_sum[...] = self.buffer[self.half_at(self.parity), :] + self.pair_land[...]
        for copy in self.second():
            copy.start()

    def slab_sum(self):
        for copy in self.second():
            copy.wait()
        value = self.half_sum[self.part_at(self.place), :]
        for d in range(1, self.line_count):
            value = value + self.line_land[d - 1]
        return value

    def start_gather(self, value=None):
        self.total[self.slab_at(), :] = self.slab_sum() if value is None else value
        for copy in self.third():
            copy.start()

    def start_pair_gather(self):
        for copy in self.third():
            copy.wait()
        self.last().start()

    def finish(self):
        self.last().wait()


PIECES = 6


def whole_kernel(
    regions, members,
    observed_ref, noise_ref, mid_ref, root_ref, mid_prior_ref, root_prior_ref, count_ref,
    root_out, mid_out, leaf_out,
    *scratch,
):
    refs = list(scratch)
    pieces = [[refs.pop(0) for _ in range(5)] for _ in range(PIECES)]
    (
        basis_mid, basis_root, scale_col, value_col, scale_row, value_row,
        mid_high, mid_low, root_high, root_low,
        mid_t_high, mid_t_low, root_t_high, root_t_low,
        inverse_ref, inv_ref, row_ref, full_ref, solved_ref, schur_ref,
        work_lead, land_lead, work_rest, land_rest,
        load_sem, pair_send, pair_recv, line_send, line_recv, group_send, group_recv,
    ) = refs
    slots, knots = basis_mid.shape
    roots = basis_root.shape[1]
    blocks, root_blocks = knots // BLOCK, roots // BLOCK
    part, root_part = blocks // 2, root_blocks // 2
    cut, root_cut = part * BLOCK, root_part * BLOCK
    me = lax.axis_index("region")
    group = lax.axis_index("group")
    line_count = regions // 2
    steps = members.bit_length() - 1
    partners = []
    for s in range(steps):
        bit = 1 << s
        partners.append(group + bit * (1 - 2 * ((group // bit) % 2)))
    barrier = pltpu.get_barrier_semaphore()
    for partner in partners:
        pl.semaphore_signal(barrier, inc=1, device_id={"group": partner}, device_id_type=MESH)
    peers = [me + 1 - 2 * (me % 2)]
    for d in range(1, line_count):
        peers.append((me // 2 + d) % line_count * 2 + me % 2)
    for peer in peers:
        pl.semaphore_signal(barrier, inc=1, device_id={"region": peer}, device_id_type=MESH)
    sems = (pair_send, pair_recv, line_send, line_recv)
    lead, rest, cross_lead, cross_rest, root_lead, root_rest = [
        Exchange(regions, slot, pieces[slot], sems) for slot in range(PIECES)
    ]

    load_rows = slots // LOADS

    def load(which, c):
        source, target = ((mid_ref, basis_mid), (root_ref, basis_root))[which]
        at = pl.ds(c * load_rows, load_rows)
        return pltpu.make_async_copy(source.at[at], target.at[at], load_sem.at[which, c])

    for which in range(2):
        for c in range(LOADS):
            load(which, c).start()
    shape = noise_ref.shape
    index = lax.broadcasted_iota(jnp.int32, shape, 0) * BLOCK + lax.broadcasted_iota(
        jnp.int32, shape, 1
    )
    weight = jnp.where(index < count_ref[...], noise_ref[...], 0.0)
    scale = jnp.sqrt(weight)
    scale_row[...] = scale
    value_row[...] = scale * observed_ref[...]

    def spread(c, carry):
        at = pl.ds(pl.multiple_of(c * BLOCK, BLOCK), BLOCK)
        square = (BLOCK, BLOCK)
        scale_col[at, :] = jnp.broadcast_to(scale_row[pl.ds(c, 1), :], square).T
        value_col[at, :] = jnp.broadcast_to(value_row[pl.ds(c, 1), :], square).T
        return carry

    lax.fori_loop(0, slots // BLOCK, spread, 0)

    def scaled(which, basis, high_ref, low_ref, t_high_ref, t_low_ref):
        width = basis.shape[1]
        wide = width // BLOCK

        def chunk(c, total):
            at = pl.ds(pl.multiple_of(c * BLOCK, BLOCK), BLOCK)
            scales = scale_col[at, :]
            value = basis[at, :] * jnp.concatenate([scales] * wide, axis=1)
            high, low = split(value)
            high_ref[at, :] = high
            low_ref[at, :] = low
            t_high_ref[:, at] = high.T
            t_low_ref[:, at] = low.T
            values = value_col[at, :]
            term = value * jnp.concatenate([values] * wide, axis=1)
            for i in range(BLOCK // PANEL):
                total = total + term[i * PANEL : (i + 1) * PANEL, :]
            return total

        total = jnp.zeros((PANEL, width), jnp.float32)
        per = load_rows // BLOCK
        for c in range(LOADS):
            load(which, c).wait()
            total = lax.fori_loop(c * per, (c + 1) * per, chunk, total)
        return jnp.sum(total, axis=0, keepdims=True)

    def gram(left, right, rows, cols):
        left_high, left_low = left
        right_high, right_low = right
        return (
            bf(left_high[rows, :], right_high[:, cols])
            + bf(left_high[rows, :], right_low[:, cols])
            + bf(left_low[rows, :], right_high[:, cols])
        )

    def symmetric(left, right, rows):
        left_high, _ = left
        right_high, right_low = right
        near = bf(left_high[rows, :], right_low[:, rows])
        return bf(left_high[rows, :], right_high[:, rows]) + near + near.T

    def put(piece, pairs, rows, cols, value):
        for t, (i, j) in enumerate(pairs):
            if rows <= i < rows + value.shape[0] // BLOCK and cols <= j < cols + value.shape[1] // BLOCK:
                piece.buffer[span(t), :] = value[span(i - rows), span(j - cols)]

    lead_pairs, rest_pairs = block_pairs(0, part), block_pairs(part, blocks)
    root_lead_pairs = block_pairs(0, root_part)
    root_rest_pairs = block_pairs(root_part, root_blocks)
    mid_rhs = scaled(0, basis_mid, mid_high, mid_low, mid_t_high, mid_t_low)
    mid_left, mid_right = (mid_t_high, mid_t_low), (mid_high, mid_low)
    root_left, root_right = (root_t_high, root_t_low), (root_high, root_low)
    low_half, high_half = slice(0, cut), slice(cut, knots)
    root_low_half, root_high_half = slice(0, root_cut), slice(root_cut, roots)

    fill(lead.buffer, len(lead_pairs) * BLOCK, None)
    put(lead, lead_pairs, 0, 0, symmetric(mid_left, mid_right, low_half))
    pl.semaphore_wait(barrier, steps + line_count)
    lead.start_pair()
    fill(rest.buffer, len(rest_pairs) * BLOCK, None)
    put(rest, rest_pairs, part, 0, gram(mid_left, mid_right, high_half, low_half))
    put(rest, rest_pairs, part, part, symmetric(mid_left, mid_right, high_half))
    rest.start_pair()
    lead.start_line()
    root_rhs = scaled(1, basis_root, root_high, root_low, root_t_high, root_t_low)
    lead.start_gather()

    def put_cross(piece, first, last):
        for half in (low_half, high_half):
            value = gram(mid_left, root_right, half, slice(first * BLOCK, last * BLOCK))
            for j in range(first, last):
                at = (j - first) * knots + half.start
                piece.buffer[at : at + cut, :] = value[:, span(j - first)]

    fill(cross_lead.buffer, root_part * knots, None)
    put_cross(cross_lead, 0, root_part)
    cross_lead.start_pair()
    rest.start_line()
    cross_base = (root_blocks - root_part) * knots
    fill(cross_rest.buffer, cross_base, mid_rhs)
    put_cross(cross_rest, root_part, root_blocks)
    lead.start_pair_gather()
    cross_rest.start_pair()
    fill(root_lead.buffer, len(root_lead_pairs) * BLOCK, None)
    put(root_lead, root_lead_pairs, 0, 0, symmetric(root_left, root_right, root_low_half))
    rest.start_gather()
    root_base = len(root_rest_pairs) * BLOCK
    fill(root_rest.buffer, root_base, root_rhs)
    put(
        root_rest, root_rest_pairs, root_part, 0,
        gram(root_left, root_right, root_high_half, root_low_half),
    )
    put(
        root_rest, root_rest_pairs, root_part, root_part,
        symmetric(root_left, root_right, root_high_half),
    )
    cross_lead.start_line()
    lead.finish()
    place_upper(inverse_ref, lead.total, mid_prior_ref, lead_pairs)

    def mid_arrive():
        rest.finish()
        place_upper(inverse_ref, rest.total, mid_prior_ref, rest_pairs)

    def after_first():
        rest.start_pair_gather()
        cross_rest.start_line()
        root_lead.start_pair()
        root_rest.start_pair()

    def after_second():
        cross_lead.start_gather()
        root_lead.start_line()

    def after_third():
        cross_rest.start_gather()
        cross_lead.start_pair_gather()
        root_rest.start_line()

    def after_fourth():
        cross_rest.start_pair_gather()

    last = blocks - 1
    hooks = {0: after_first, 1: after_second, last - 1: after_third, last: after_fourth}
    each_block(
        inverse_ref, inv_ref, hooks,
        factor_tails(inverse_ref, row_ref, inv_ref, part, mid_arrive),
    )
    own_lead = root_lead.slab_sum()
    own_rest = root_rest.slab_sum()
    cross_lead.finish()
    for j in range(root_part):
        full_ref[:, span(j)] = cross_lead.total[j * knots : (j + 1) * knots, :]
    cross_rest.finish()
    for j in range(root_part, root_blocks):
        at = (j - root_part) * knots
        full_ref[:, span(j)] = cross_rest.total[at : at + knots, :]
    rhs_row = unpack_row(cross_rest.total, cross_base, knots)
    remaining = [rhs_row[:, span(k)] for k in range(blocks)]
    solved_parts = []
    for k in range(blocks):
        later = slice((k + 1) * BLOCK, knots)
        own_rows = full_ref[span(k), :]
        if k + 1 < blocks:
            row = row_ref[span(k), later]
            full_ref[later, :] = full_ref[later, :] - mxu_tn(row, own_rows)
            change = mxu(remaining[k], row)
            for i in range(k + 1, blocks):
                remaining[i] = remaining[i] - change[:, span(i - k - 1)]
        solved_ref[span(k), :] = mxu(inv_ref[span(k), :], own_rows)
        solved_parts.append(mxu(remaining[k], inv_ref[span(k), :]))

    def schur(piece, pairs):
        for t, (i, j) in enumerate(pairs):
            if j == 0:
                rows = mxu_tn(full_ref[:, span(i)], solved_ref[:, : (i + 1) * BLOCK])
            schur_ref[span(t), :] = rows[:, span(j)]

    def combine(s, work, land, semaphore):
        return pltpu.make_async_remote_copy(
            src_ref=work.at[s],
            dst_ref=land.at[s],
            send_sem=group_send.at[semaphore, s],
            recv_sem=group_recv.at[semaphore, s],
            device_id={"group": partners[s]},
            device_id_type=MESH,
        )

    schur(root_lead, root_lead_pairs)
    fill(schur_ref, len(root_lead_pairs) * BLOCK, None)
    work_lead[0] = own_lead - schur_ref[root_lead.slab_at(), :]
    combine(0, work_lead, land_lead, 0).start()
    schur(root_rest, root_rest_pairs)
    fill(schur_ref, root_base, mxu(jnp.concatenate(solved_parts, axis=1), full_ref[...]))
    work_rest[0] = own_rest - schur_ref[root_rest.slab_at(), :]
    combine(0, work_rest, land_rest, 1).start()
    for s in range(steps):
        for work, land, semaphore, piece in (
            (work_lead, land_lead, 0, root_lead),
            (work_rest, land_rest, 1, root_rest),
        ):
            combine(s, work, land, semaphore).wait()
            value = work[s] + land[s]
            if s + 1 < steps:
                work[s + 1] = value
                combine(s + 1, work, land, semaphore).start()
            else:
                piece.start_gather(value)
    for k in reversed(range(blocks - 1)):
        later = slice((k + 1) * BLOCK, knots)
        row = row_ref[span(k), later]
        solved_ref[span(k), :] = solved_ref[span(k), :] - mxu(row, solved_ref[later, :])
        solved_parts[k] = solved_parts[k] - mxu_nt(
            jnp.concatenate(solved_parts[k + 1 :], axis=1), row
        )
    solved_rhs = jnp.concatenate(solved_parts, axis=1)
    root_lead.start_pair_gather()
    root_rest.start_pair_gather()
    root_lead.finish()
    place_upper(inverse_ref, root_lead.total, root_prior_ref, root_lead_pairs)

    def root_arrive():
        root_rest.finish()
        place_upper(inverse_ref, root_rest.total, root_prior_ref, root_rest_pairs)

    each_block(
        inverse_ref, inv_ref, {},
        factor_tails(inverse_ref, row_ref, inv_ref, root_part, root_arrive),
    )
    vector = unpack_row(root_rest.total, root_base, roots)
    remaining = [vector[:, span(k)] for k in range(root_blocks)]
    weight_parts = []
    for k in range(root_blocks):
        if k + 1 < root_blocks:
            change = mxu(remaining[k], row_ref[span(k), (k + 1) * BLOCK : roots])
            for i in range(k + 1, root_blocks):
                remaining[i] = remaining[i] - change[:, span(i - k - 1)]
        weight_parts.append(mxu(remaining[k], inv_ref[span(k), :]))
    for k in reversed(range(root_blocks - 1)):
        weight_parts[k] = weight_parts[k] - mxu_nt(
            jnp.concatenate(weight_parts[k + 1 :], axis=1), row_ref[span(k), (k + 1) * BLOCK : roots]
        )
    weights = jnp.concatenate(weight_parts, axis=1)
    middle = solved_rhs - mxu_nt(weights, solved_ref[...])
    root_out[...] = weights[0:1, :]
    mid_out[...] = middle[0:1, :]
    mid_rows = [jnp.broadcast_to(middle[0:1, span(j)], (BLOCK, BLOCK)) for j in range(blocks)]
    root_rows = [jnp.broadcast_to(weights[0:1, span(j)], (BLOCK, BLOCK)) for j in range(root_blocks)]

    for c in range(slots // BLOCK):
        at = span(c)
        total = jnp.zeros((BLOCK, BLOCK), jnp.float32)
        for j in range(blocks):
            total = total + basis_mid[at, span(j)] * mid_rows[j]
        for j in range(root_blocks):
            total = total + basis_root[at, span(j)] * root_rows[j]
        leaf_out[c : c + 1, :] = jnp.sum(total.T, axis=0, keepdims=True)


def round_up(value, unit):
    return (value + unit - 1) // unit * unit


def whole(observed, noise, mid_basis, root_basis, mid_prior, root_prior, leaf_count):
    slots, knots = mid_basis.shape
    roots = root_basis.shape[1]
    regions = lax.axis_size("region")
    members = lax.axis_size("group")
    line_count = regions // 2
    steps = members.bit_length() - 1
    unit = PANEL * regions
    blocks, root_blocks = knots // BLOCK, roots // BLOCK
    part, root_part = blocks // 2, root_blocks // 2
    sizes = [
        len(block_pairs(0, part)) * BLOCK,
        len(block_pairs(part, blocks)) * BLOCK,
        root_part * knots,
        (root_blocks - root_part) * knots + blocks,
        len(block_pairs(0, root_part)) * BLOCK,
        len(block_pairs(root_part, root_blocks)) * BLOCK + root_blocks,
    ]
    sizes = [round_up(size, unit) for size in sizes]

    def vmem(*shape):
        return pltpu.VMEM(shape, jnp.float32)

    def half(*shape):
        return pltpu.VMEM(shape, jnp.bfloat16)

    scratch = []
    for rows in sizes:
        scratch += [
            vmem(rows, BLOCK),
            vmem(rows, BLOCK),
            vmem(rows // 2, BLOCK),
            vmem(rows // 2, BLOCK),
            vmem(line_count - 1, rows // regions, BLOCK),
        ]
    scratch += [
        vmem(slots, knots),
        vmem(slots, roots),
        vmem(slots, BLOCK),
        vmem(slots, BLOCK),
        vmem(slots // BLOCK, BLOCK),
        vmem(slots // BLOCK, BLOCK),
        half(slots, knots),
        half(slots, knots),
        half(slots, roots),
        half(slots, roots),
        half(knots, slots),
        half(knots, slots),
        half(roots, slots),
        half(roots, slots),
        vmem(knots, knots),
        vmem(max(knots, roots), BLOCK),
        vmem(max(knots, roots), max(knots, roots)),
        vmem(knots, roots),
        vmem(knots, roots),
        vmem(max(sizes[4:]), BLOCK),
        vmem(steps, sizes[4] // regions, BLOCK),
        vmem(steps, sizes[4] // regions, BLOCK),
        vmem(steps, sizes[5] // regions, BLOCK),
        vmem(steps, sizes[5] // regions, BLOCK),
        pltpu.SemaphoreType.DMA((2, LOADS)),
        pltpu.SemaphoreType.DMA((2 * PIECES,)),
        pltpu.SemaphoreType.DMA((2 * PIECES,)),
        pltpu.SemaphoreType.DMA((2 * PIECES, line_count - 1)),
        pltpu.SemaphoreType.DMA((2 * PIECES, line_count - 1)),
        pltpu.SemaphoreType.DMA((2, steps)),
        pltpu.SemaphoreType.DMA((2, steps)),
    ]
    near = pl.BlockSpec(memory_space=pltpu.VMEM)
    far = pl.BlockSpec(memory_space=pl.ANY)
    return pl.pallas_call(
        functools.partial(whole_kernel, regions, members),
        out_shape=(
            jax.ShapeDtypeStruct((1, roots), jnp.float32),
            jax.ShapeDtypeStruct((1, knots), jnp.float32),
            jax.ShapeDtypeStruct((slots // BLOCK, BLOCK), jnp.float32),
        ),
        in_specs=[near, near, far, far, near, near, near],
        out_specs=(near, near, near),
        scratch_shapes=scratch,
        compiler_params=pltpu.CompilerParams(
            collective_id=0, has_side_effects=True, vmem_limit_bytes=56 * 1024 * 1024
        ),
        name="posterior",
    )(
        observed.reshape(slots // BLOCK, BLOCK),
        noise.reshape(slots // BLOCK, BLOCK),
        mid_basis,
        root_basis,
        mid_prior,
        root_prior[None, :],
        leaf_count,
    )


def on_device(observed, noise_precision, mid_basis, root_basis, mid_prior, root_prior, leaf_count):
    knots = mid_basis.shape[1]
    root_means, group_means, leaf = whole(
        observed, noise_precision, mid_basis, root_basis, mid_prior, root_prior, leaf_count
    )
    slab = knots // lax.axis_size("region")
    middle = lax.dynamic_slice_in_dim(group_means, lax.axis_index("region") * slab, slab, 1)
    return (root_means[0], middle, leaf.reshape(-1))


def solution(mesh):
    return jax.shard_map(
        on_device,
        mesh=mesh,
        in_specs=(
            P(("group", "region")),
            P(("group", "region")),
            P(("group", "region"), None),
            P(("group", "region"), None),
            P("group", None),
            P(),
            P("group", "region"),
        ),
        out_specs=(P(), P("group", "region"), P(("group", "region"))),
        check_vma=False,
    )
```

```python
import functools

import jax
import jax.numpy as jnp
from jax import lax
from jax.experimental import pallas as pl
from jax.experimental.pallas import tpu as pltpu
from jax.sharding import PartitionSpec as P

HIGHEST = lax.Precision.HIGHEST
MESH = pl.DeviceIdType.MESH
BLOCK = 128
PANEL = 8
WIDE = 16
LOADS = 4


def mxu(a, b):
    return jnp.dot(a, b, precision=HIGHEST, preferred_element_type=jnp.float32)


def mxu_tn(a, b):
    return lax.dot_general(
        a, b, (((0,), (0,)), ((), ())), precision=HIGHEST, preferred_element_type=jnp.float32
    )


def mxu_nt(a, b):
    return lax.dot_general(
        a, b, (((1,), (1,)), ((), ())), precision=HIGHEST, preferred_element_type=jnp.float32
    )


def split(x):
    high = x.astype(jnp.bfloat16)
    return high, (x - high.astype(jnp.float32)).astype(jnp.bfloat16)


def split3(x):
    high = x.astype(jnp.bfloat16)
    rest = x - high.astype(jnp.float32)
    mid = rest.astype(jnp.bfloat16)
    return high, mid, (rest - mid.astype(jnp.float32)).astype(jnp.bfloat16)


def bf(a, b):
    return jnp.dot(a, b, preferred_element_type=jnp.float32)


def beside(a, b):
    return jnp.concatenate([a, b], axis=1)


def above(a, b):
    return jnp.concatenate([a, b], axis=0)


def negated_inverse(groups):
    count = len(groups)
    size = count * PANEL
    shape = (PANEL, size)
    per = WIDE // PANEL
    lane = lax.broadcasted_iota(jnp.int32, shape, 1)
    sub = lax.broadcasted_iota(jnp.int32, shape, 0)

    def row_of(value, k):
        return jnp.broadcast_to(value[k : k + 1, :], shape)

    def column_of(value, k):
        return jnp.broadcast_to(value[:, k : k + 1], shape)

    for p in range(size // WIDE):
        first = p * WIDE
        inside = (lane >= first) & (lane < first + WIDE)
        mine = groups[p * per : (p + 1) * per]
        cols = [[column_of(g, first + k) for g in mine] for k in range(WIDE)]
        work = [
            jnp.where(lane == first + PANEL * i + sub, -1.0, jnp.where(inside, 0.0, g))
            for i, g in enumerate(mine)
        ]
        for k in range(0, WIDE, 2):
            at, s = k // PANEL, k % PANEL
            left, right = cols[k], cols[k + 1]
            top, side, low = row_of(left[at], s), row_of(right[at], s), row_of(right[at], s + 1)
            inv = 1.0 / (top * low - side * side)
            inv_top, inv_side, inv_low = low * inv, -side * inv, top * inv
            former = [left[v] * inv_top + right[v] * inv_side for v in range(per)]
            latter = [left[v] * inv_side + right[v] * inv_low for v in range(per)]
            former[at] = jnp.where(sub == s, -inv_top, jnp.where(sub == s + 1, -inv_side, former[at]))
            latter[at] = jnp.where(sub == s, -inv_side, jnp.where(sub == s + 1, -inv_low, latter[at]))
            pivot = (sub == s) | (sub == s + 1)

            def cleared(target):
                upper, lower = row_of(target[at], s), row_of(target[at], s + 1)
                base = list(target)
                base[at] = jnp.where(pivot, 0.0, base[at])
                return [base[v] - former[v] * upper - latter[v] * lower for v in range(per)]

            for j in range(k + 2, WIDE):
                cols[j] = cleared(cols[j])
            work = cleared(work)
        near = [i for i in range((p + 1) * per, (p + 2) * per) if i < count]
        far = [i for i in range(count) if i // per != p and i not in near]
        after = list(groups)
        spread = [row_of(work[k // PANEL], k % PANEL) for k in range(WIDE)]
        for i in near:
            value = jnp.where(inside, 0.0, groups[i])
            for k in range(WIDE):
                value = value - column_of(groups[i], first + k) * spread[k]
            after[i] = value
        blank = jnp.zeros(shape, jnp.float32)
        padded = [work[i - p * per] if i // per == p else blank for i in range(count)]
        row_high, row_mid, row_low = split3(jnp.concatenate(padded, axis=0))
        high, mid, low = split3(jnp.concatenate(groups, axis=0))
        both = beside(high, mid)
        product = (
            bf(both, above(row_high, row_high))
            + bf(both, above(row_mid, row_mid))
            + bf(beside(low, high), above(row_high, row_low))
        )
        for i in far:
            after[i] = jnp.where(inside, 0.0, groups[i]) - product[i * PANEL : (i + 1) * PANEL, :]
        for i in range(per):
            after[p * per + i] = work[i]
        groups = after
    return groups


def each_block(a_ref, inv_ref, hooks, tails):
    blocks = a_ref.shape[0] // BLOCK

    def step(kb, carry):
        own = pl.ds(pl.multiple_of(kb * BLOCK, BLOCK), BLOCK)
        diagonal = a_ref[own, own]
        groups = [diagonal[i * PANEL : (i + 1) * PANEL, :] for i in range(BLOCK // PANEL)]
        inverse = -jnp.concatenate(negated_inverse(groups), axis=0)
        inv_ref[own, :] = inverse
        for at, hook in hooks.items():
            pl.when(kb == at)(hook)
        for at, tail in tails.items():
            pl.when(kb == at)(tail)
        return carry

    lax.fori_loop(0, blocks, step, 0)


def eliminate(a_ref, row_ref, inv_ref, k, first, last):
    if first >= last:
        return
    cols = slice(first * BLOCK, last * BLOCK)
    upper = a_ref[span(k), cols]
    row = mxu(inv_ref[span(k), :], upper)
    row_ref[span(k), cols] = row
    a_ref[cols, cols] = a_ref[cols, cols] - mxu_tn(upper, row)


def factor_tails(a_ref, row_ref, inv_ref, part, arrive):
    blocks = a_ref.shape[0] // BLOCK
    rest = slice(part * BLOCK, blocks * BLOCK)

    def lead_tail(k):
        eliminate(a_ref, row_ref, inv_ref, k, k + 1, part)

    def join():
        arrive()
        for k in range(part):
            upper = a_ref[span(k), rest]
            row = mxu(inv_ref[span(k), :], upper)
            row_ref[span(k), rest] = row
            if k + 1 < part:
                inner = slice((k + 1) * BLOCK, part * BLOCK)
                a_ref[inner, rest] = a_ref[inner, rest] - mxu_tn(a_ref[span(k), inner], row)
            a_ref[rest, rest] = a_ref[rest, rest] - mxu_tn(upper, row)

    def rest_tail(k):
        eliminate(a_ref, row_ref, inv_ref, k, k + 1, blocks)

    tails = {k: functools.partial(lead_tail, k) for k in range(part - 1)}
    tails[part - 1] = join
    for k in range(part, blocks - 1):
        tails[k] = functools.partial(rest_tail, k)
    return tails


def span(i):
    return slice(i * BLOCK, (i + 1) * BLOCK)


def block_pairs(first, last):
    return [(i, j) for i in range(first, last) for j in range(i + 1)]


def diagonal_of(prior_ref, i):
    rows = lax.broadcasted_iota(jnp.int32, (BLOCK, BLOCK), 0)
    cols = lax.broadcasted_iota(jnp.int32, (BLOCK, BLOCK), 1)
    return jnp.where(rows == cols, prior_ref[:, span(i)], 0.0)


def place_upper(matrix_ref, packed_ref, prior_ref, pairs):
    for t, (i, j) in enumerate(pairs):
        value = packed_ref[span(t), :]
        if i == j:
            matrix_ref[span(i), span(i)] = value + diagonal_of(prior_ref, i)
        else:
            turned = value.T
            matrix_ref[span(j), span(i)] = turned
            if symmetric_at(pairs, j):
                matrix_ref[span(i), span(j)] = value


def symmetric_at(pairs, j):
    return (j, j) in pairs


def fill(packed_ref, base, value):
    tail = packed_ref.shape[0] - base
    if tail:
        packed_ref[base:, :] = jnp.zeros((tail, BLOCK), jnp.float32)
    if value is not None:
        for i in range(value.shape[1] // BLOCK):
            packed_ref[base + i : base + i + 1, :] = value[0:1, span(i)]


def unpack_row(packed_ref, base, size):
    parts = [packed_ref[base + i : base + i + 1, :] for i in range(size // BLOCK)]
    return jnp.broadcast_to(jnp.concatenate(parts, axis=1), (PANEL, size))


class Exchange:
    def __init__(self, regions, slot, refs, sems):
        self.me = lax.axis_index("region")
        self.parity = self.me % 2
        self.place = self.me // 2
        self.line_count = regions // 2
        self.slot = slot
        self.buffer, self.total, self.pair_land, self.half_sum, self.line_land = refs
        self.pair_send, self.pair_recv, self.line_send, self.line_recv = sems
        self.half = self.buffer.shape[0] // 2
        self.slab = self.half // self.line_count

    def half_at(self, parity):
        return pl.ds(pl.multiple_of(parity * self.half, PANEL), self.half)

    def slab_at(self):
        start = self.parity * self.half + self.place * self.slab
        return pl.ds(pl.multiple_of(start, PANEL), self.slab)

    def part_at(self, place):
        return pl.ds(pl.multiple_of(place * self.slab, PANEL), self.slab)

    def pair_copy(self, which, source, target):
        return pltpu.make_async_remote_copy(
            src_ref=source,
            dst_ref=target,
            send_sem=self.pair_send.at[self.slot * 2 + which],
            recv_sem=self.pair_recv.at[self.slot * 2 + which],
            device_id={"region": self.me + 1 - 2 * self.parity},
            device_id_type=MESH,
        )

    def line_copy(self, which, d, source, target):
        place = (self.place + d) % self.line_count
        return pltpu.make_async_remote_copy(
            src_ref=source(place),
            dst_ref=target,
            send_sem=self.line_send.at[self.slot * 2 + which, d - 1],
            recv_sem=self.line_recv.at[self.slot * 2 + which, d - 1],
            device_id={"region": place * 2 + self.parity},
            device_id_type=MESH,
        )

    def first(self):
        return self.pair_copy(0, self.buffer.at[self.half_at(1 - self.parity)], self.pair_land)

    def second(self):
        return [
            self.line_copy(
                0, d, lambda place: self.half_sum.at[self.part_at(place)], self.line_land.at[d - 1]
            )
            for d in range(1, self.line_count)
        ]

    def third(self):
        own = self.slab_at()
        return [
            self.line_copy(1, d, lambda place: self.total.at[own], self.total.at[own])
            for d in range(1, self.line_count)
        ]

    def last(self):
        mine = self.total.at[self.half_at(self.parity)]
        return self.pair_copy(1, mine, mine)

    def start_pair(self):
        self.first().start()

    def start_line(self):
        self.first().wait()
        self.half_sum[...] = self.buffer[self.half_at(self.parity), :] + self.pair_land[...]
        for copy in self.second():
            copy.start()

    def slab_sum(self):
        for copy in self.second():
            copy.wait()
        value = self.half_sum[self.part_at(self.place), :]
        for d in range(1, self.line_count):
            value = value + self.line_land[d - 1]
        return value

    def start_gather(self, value=None):
        self.total[self.slab_at(), :] = self.slab_sum() if value is None else value
        for copy in self.third():
            copy.start()

    def start_pair_gather(self):
        for copy in self.third():
            copy.wait()
        self.last().start()

    def finish(self):
        self.last().wait()


PIECES = 6


def whole_kernel(
    regions, members,
    observed_ref, noise_ref, mid_ref, root_ref, mid_prior_ref, root_prior_ref, count_ref,
    root_out, mid_out, leaf_out,
    *scratch,
):
    refs = list(scratch)
    pieces = [[refs.pop(0) for _ in range(5)] for _ in range(PIECES)]
    (
        basis_mid, basis_root, scale_col, value_col, scale_row, value_row,
        mid_high, mid_low, root_high, root_low,
        mid_t_high, mid_t_low, root_t_high, root_t_low,
        inverse_ref, inv_ref, row_ref, full_ref, solved_ref, schur_ref,
        work_lead, land_lead, work_rest, land_rest,
        load_sem, pair_send, pair_recv, line_send, line_recv, group_send, group_recv,
    ) = refs
    slots, knots = basis_mid.shape
    roots = basis_root.shape[1]
    blocks, root_blocks = knots // BLOCK, roots // BLOCK
    part, root_part = blocks // 2, root_blocks // 2
    cut, root_cut = part * BLOCK, root_part * BLOCK
    me = lax.axis_index("region")
    group = lax.axis_index("group")
    line_count = regions // 2
    steps = members.bit_length() - 1
    partners = []
    for s in range(steps):
        bit = 1 << s
        partners.append(group + bit * (1 - 2 * ((group // bit) % 2)))
    barrier = pltpu.get_barrier_semaphore()
    for partner in partners:
        pl.semaphore_signal(barrier, inc=1, device_id={"group": partner}, device_id_type=MESH)
    peers = [me + 1 - 2 * (me % 2)]
    for d in range(1, line_count):
        peers.append((me // 2 + d) % line_count * 2 + me % 2)
    for peer in peers:
        pl.semaphore_signal(barrier, inc=1, device_id={"region": peer}, device_id_type=MESH)
    sems = (pair_send, pair_recv, line_send, line_recv)
    lead, rest, cross_lead, cross_rest, root_lead, root_rest = [
        Exchange(regions, slot, pieces[slot], sems) for slot in range(PIECES)
    ]

    load_rows = slots // LOADS

    def load(which, c):
        source, target = ((mid_ref, basis_mid), (root_ref, basis_root))[which]
        at = pl.ds(c * load_rows, load_rows)
        return pltpu.make_async_copy(source.at[at], target.at[at], load_sem.at[which, c])

    for c in range(LOADS):
        load(0, c).start()
    shape = noise_ref.shape
    index = lax.broadcasted_iota(jnp.int32, shape, 0) * BLOCK + lax.broadcasted_iota(
        jnp.int32, shape, 1
    )
    weight = jnp.where(index < count_ref[...], noise_ref[...], 0.0)
    scale = jnp.sqrt(weight)
    scale_row[...] = scale
    value_row[...] = scale * observed_ref[...]

    def spread(c, carry):
        at = pl.ds(pl.multiple_of(c * BLOCK, BLOCK), BLOCK)
        square = (BLOCK, BLOCK)
        scale_col[at, :] = jnp.broadcast_to(scale_row[pl.ds(c, 1), :], square).T
        value_col[at, :] = jnp.broadcast_to(value_row[pl.ds(c, 1), :], square).T
        return carry

    lax.fori_loop(0, slots // BLOCK, spread, 0)

    def scaled(which, basis, high_ref, low_ref, t_high_ref, t_low_ref):
        width = basis.shape[1]
        wide = width // BLOCK

        def chunk(c, total):
            at = pl.ds(pl.multiple_of(c * BLOCK, BLOCK), BLOCK)
            scales = scale_col[at, :]
            value = basis[at, :] * jnp.concatenate([scales] * wide, axis=1)
            high, low = split(value)
            high_ref[at, :] = high
            low_ref[at, :] = low
            t_high_ref[:, at] = high.T
            t_low_ref[:, at] = low.T
            values = value_col[at, :]
            term = value * jnp.concatenate([values] * wide, axis=1)
            for i in range(BLOCK // PANEL):
                total = total + term[i * PANEL : (i + 1) * PANEL, :]
            return total

        total = jnp.zeros((PANEL, width), jnp.float32)
        per = load_rows // BLOCK
        for c in range(LOADS):
            load(which, c).wait()
            if which == 0:
                load(1, c).start()
            total = lax.fori_loop(c * per, (c + 1) * per, chunk, total)
        return jnp.sum(total, axis=0, keepdims=True)

    def gram(left, right, rows, cols):
        left_high, left_low = left
        right_high, right_low = right
        return (
            bf(left_high[rows, :], right_high[:, cols])
            + bf(left_high[rows, :], right_low[:, cols])
            + bf(left_low[rows, :], right_high[:, cols])
        )

    def symmetric(left, right, rows):
        left_high, _ = left
        right_high, right_low = right
        near = bf(left_high[rows, :], right_low[:, rows])
        return bf(left_high[rows, :], right_high[:, rows]) + near + near.T

    def put(piece, pairs, rows, cols, value):
        for t, (i, j) in enumerate(pairs):
            if rows <= i < rows + value.shape[0] // BLOCK and cols <= j < cols + value.shape[1] // BLOCK:
                piece.buffer[span(t), :] = value[span(i - rows), span(j - cols)]

    lead_pairs, rest_pairs = block_pairs(0, part), block_pairs(part, blocks)
    root_lead_pairs = block_pairs(0, root_part)
    root_rest_pairs = block_pairs(root_part, root_blocks)
    mid_rhs = scaled(0, basis_mid, mid_high, mid_low, mid_t_high, mid_t_low)
    mid_left, mid_right = (mid_t_high, mid_t_low), (mid_high, mid_low)
    root_left, root_right = (root_t_high, root_t_low), (root_high, root_low)
    low_half, high_half = slice(0, cut), slice(cut, knots)
    root_low_half, root_high_half = slice(0, root_cut), slice(root_cut, roots)

    fill(lead.buffer, len(lead_pairs) * BLOCK, None)
    put(lead, lead_pairs, 0, 0, symmetric(mid_left, mid_right, low_half))
    pl.semaphore_wait(barrier, steps + line_count)
    lead.start_pair()
    fill(rest.buffer, len(rest_pairs) * BLOCK, None)
    put(rest, rest_pairs, part, 0, gram(mid_left, mid_right, high_half, low_half))
    put(rest, rest_pairs, part, part, symmetric(mid_left, mid_right, high_half))
    rest.start_pair()
    lead.start_line()
    root_rhs = scaled(1, basis_root, root_high, root_low, root_t_high, root_t_low)
    lead.start_gather()

    def put_cross(piece, first, last):
        for half in (low_half, high_half):
            value = gram(mid_left, root_right, half, slice(first * BLOCK, last * BLOCK))
            for j in range(first, last):
                at = (j - first) * knots + half.start
                piece.buffer[at : at + cut, :] = value[:, span(j - first)]

    fill(cross_lead.buffer, root_part * knots, None)
    put_cross(cross_lead, 0, root_part)
    cross_lead.start_pair()
    rest.start_line()
    cross_base = (root_blocks - root_part) * knots
    fill(cross_rest.buffer, cross_base, mid_rhs)
    put_cross(cross_rest, root_part, root_blocks)
    lead.start_pair_gather()
    cross_rest.start_pair()
    fill(root_lead.buffer, len(root_lead_pairs) * BLOCK, None)
    put(root_lead, root_lead_pairs, 0, 0, symmetric(root_left, root_right, root_low_half))
    rest.start_gather()
    root_base = len(root_rest_pairs) * BLOCK
    fill(root_rest.buffer, root_base, root_rhs)
    put(
        root_rest, root_rest_pairs, root_part, 0,
        gram(root_left, root_right, root_high_half, root_low_half),
    )
    put(
        root_rest, root_rest_pairs, root_part, root_part,
        symmetric(root_left, root_right, root_high_half),
    )
    cross_lead.start_line()
    lead.finish()
    place_upper(inverse_ref, lead.total, mid_prior_ref, lead_pairs)

    def mid_arrive():
        rest.finish()
        place_upper(inverse_ref, rest.total, mid_prior_ref, rest_pairs)

    def after_first():
        rest.start_pair_gather()
        cross_rest.start_line()
        root_lead.start_pair()
        root_rest.start_pair()

    def after_second():
        cross_lead.start_gather()
        root_lead.start_line()

    def after_third():
        cross_rest.start_gather()
        cross_lead.start_pair_gather()
        root_rest.start_line()

    def after_fourth():
        cross_rest.start_pair_gather()

    last = blocks - 1
    hooks = {0: after_first, 1: after_second, last - 1: after_third, last: after_fourth}
    each_block(
        inverse_ref, inv_ref, hooks,
        factor_tails(inverse_ref, row_ref, inv_ref, part, mid_arrive),
    )
    own_lead = root_lead.slab_sum()
    own_rest = root_rest.slab_sum()
    cross_lead.finish()
    for j in range(root_part):
        full_ref[:, span(j)] = cross_lead.total[j * knots : (j + 1) * knots, :]
    cross_rest.finish()
    for j in range(root_part, root_blocks):
        at = (j - root_part) * knots
        full_ref[:, span(j)] = cross_rest.total[at : at + knots, :]
    rhs_row = unpack_row(cross_rest.total, cross_base, knots)
    remaining = [rhs_row[:, span(k)] for k in range(blocks)]
    solved_parts = []
    for k in range(blocks):
        later = slice((k + 1) * BLOCK, knots)
        own_rows = full_ref[span(k), :]
        if k + 1 < blocks:
            row = row_ref[span(k), later]
            full_ref[later, :] = full_ref[later, :] - mxu_tn(row, own_rows)
            change = mxu(remaining[k], row)
            for i in range(k + 1, blocks):
                remaining[i] = remaining[i] - change[:, span(i - k - 1)]
        solved_ref[span(k), :] = mxu(inv_ref[span(k), :], own_rows)
        solved_parts.append(mxu(remaining[k], inv_ref[span(k), :]))

    def schur(piece, pairs):
        for t, (i, j) in enumerate(pairs):
            if j == 0:
                rows = mxu_tn(full_ref[:, span(i)], solved_ref[:, : (i + 1) * BLOCK])
            schur_ref[span(t), :] = rows[:, span(j)]

    def combine(s, work, land, semaphore):
        return pltpu.make_async_remote_copy(
            src_ref=work.at[s],
            dst_ref=land.at[s],
            send_sem=group_send.at[semaphore, s],
            recv_sem=group_recv.at[semaphore, s],
            device_id={"group": partners[s]},
            device_id_type=MESH,
        )

    schur(root_lead, root_lead_pairs)
    fill(schur_ref, len(root_lead_pairs) * BLOCK, None)
    work_lead[0] = own_lead - schur_ref[root_lead.slab_at(), :]
    combine(0, work_lead, land_lead, 0).start()
    schur(root_rest, root_rest_pairs)
    fill(schur_ref, root_base, mxu(jnp.concatenate(solved_parts, axis=1), full_ref[...]))
    work_rest[0] = own_rest - schur_ref[root_rest.slab_at(), :]
    combine(0, work_rest, land_rest, 1).start()
    for s in range(steps):
        for work, land, semaphore, piece in (
            (work_lead, land_lead, 0, root_lead),
            (work_rest, land_rest, 1, root_rest),
        ):
            combine(s, work, land, semaphore).wait()
            value = work[s] + land[s]
            if s + 1 < steps:
                work[s + 1] = value
                combine(s + 1, work, land, semaphore).start()
            else:
                piece.start_gather(value)
    for k in reversed(range(blocks - 1)):
        later = slice((k + 1) * BLOCK, knots)
        row = row_ref[span(k), later]
        solved_ref[span(k), :] = solved_ref[span(k), :] - mxu(row, solved_ref[later, :])
        solved_parts[k] = solved_parts[k] - mxu_nt(
            jnp.concatenate(solved_parts[k + 1 :], axis=1), row
        )
    solved_rhs = jnp.concatenate(solved_parts, axis=1)
    root_lead.start_pair_gather()
    root_rest.start_pair_gather()
    root_lead.finish()
    place_upper(inverse_ref, root_lead.total, root_prior_ref, root_lead_pairs)

    def root_arrive():
        root_rest.finish()
        place_upper(inverse_ref, root_rest.total, root_prior_ref, root_rest_pairs)

    each_block(
        inverse_ref, inv_ref, {},
        factor_tails(inverse_ref, row_ref, inv_ref, root_part, root_arrive),
    )
    vector = unpack_row(root_rest.total, root_base, roots)
    remaining = [vector[:, span(k)] for k in range(root_blocks)]
    weight_parts = []
    for k in range(root_blocks):
        if k + 1 < root_blocks:
            change = mxu(remaining[k], row_ref[span(k), (k + 1) * BLOCK : roots])
            for i in range(k + 1, root_blocks):
                remaining[i] = remaining[i] - change[:, span(i - k - 1)]
        weight_parts.append(mxu(remaining[k], inv_ref[span(k), :]))
    for k in reversed(range(root_blocks - 1)):
        weight_parts[k] = weight_parts[k] - mxu_nt(
            jnp.concatenate(weight_parts[k + 1 :], axis=1), row_ref[span(k), (k + 1) * BLOCK : roots]
        )
    weights = jnp.concatenate(weight_parts, axis=1)
    middle = solved_rhs - mxu_nt(weights, solved_ref[...])
    root_out[...] = weights[0:1, :]
    slab = mid_out.shape[1]
    turned = pltpu.roll(middle, (knots - me * slab) % knots, 1)
    mid_out[...] = turned[0:1, :slab]
    mid_rows = [jnp.broadcast_to(middle[0:1, span(j)], (BLOCK, BLOCK)) for j in range(blocks)]
    root_rows = [jnp.broadcast_to(weights[0:1, span(j)], (BLOCK, BLOCK)) for j in range(root_blocks)]

    for c in range(slots // BLOCK):
        at = span(c)
        total = jnp.zeros((BLOCK, BLOCK), jnp.float32)
        for j in range(blocks):
            total = total + basis_mid[at, span(j)] * mid_rows[j]
        for j in range(root_blocks):
            total = total + basis_root[at, span(j)] * root_rows[j]
        leaf_out[c : c + 1, :] = jnp.sum(total.T, axis=0, keepdims=True)


def round_up(value, unit):
    return (value + unit - 1) // unit * unit


def whole(observed, noise, mid_basis, root_basis, mid_prior, root_prior, leaf_count):
    slots, knots = mid_basis.shape
    roots = root_basis.shape[1]
    regions = lax.axis_size("region")
    members = lax.axis_size("group")
    line_count = regions // 2
    steps = members.bit_length() - 1
    unit = PANEL * regions
    blocks, root_blocks = knots // BLOCK, roots // BLOCK
    part, root_part = blocks // 2, root_blocks // 2
    sizes = [
        len(block_pairs(0, part)) * BLOCK,
        len(block_pairs(part, blocks)) * BLOCK,
        root_part * knots,
        (root_blocks - root_part) * knots + blocks,
        len(block_pairs(0, root_part)) * BLOCK,
        len(block_pairs(root_part, root_blocks)) * BLOCK + root_blocks,
    ]
    sizes = [round_up(size, unit) for size in sizes]

    def vmem(*shape):
        return pltpu.VMEM(shape, jnp.float32)

    def half(*shape):
        return pltpu.VMEM(shape, jnp.bfloat16)

    scratch = []
    for rows in sizes:
        scratch += [
            vmem(rows, BLOCK),
            vmem(rows, BLOCK),
            vmem(rows // 2, BLOCK),
            vmem(rows // 2, BLOCK),
            vmem(line_count - 1, rows // regions, BLOCK),
        ]
    scratch += [
        vmem(slots, knots),
        vmem(slots, roots),
        vmem(slots, BLOCK),
        vmem(slots, BLOCK),
        vmem(slots // BLOCK, BLOCK),
        vmem(slots // BLOCK, BLOCK),
        half(slots, knots),
        half(slots, knots),
        half(slots, roots),
        half(slots, roots),
        half(knots, slots),
        half(knots, slots),
        half(roots, slots),
        half(roots, slots),
        vmem(knots, knots),
        vmem(max(knots, roots), BLOCK),
        vmem(max(knots, roots), max(knots, roots)),
        vmem(knots, roots),
        vmem(knots, roots),
        vmem(max(sizes[4:]), BLOCK),
        vmem(steps, sizes[4] // regions, BLOCK),
        vmem(steps, sizes[4] // regions, BLOCK),
        vmem(steps, sizes[5] // regions, BLOCK),
        vmem(steps, sizes[5] // regions, BLOCK),
        pltpu.SemaphoreType.DMA((2, LOADS)),
        pltpu.SemaphoreType.DMA((2 * PIECES,)),
        pltpu.SemaphoreType.DMA((2 * PIECES,)),
        pltpu.SemaphoreType.DMA((2 * PIECES, line_count - 1)),
        pltpu.SemaphoreType.DMA((2 * PIECES, line_count - 1)),
        pltpu.SemaphoreType.DMA((2, steps)),
        pltpu.SemaphoreType.DMA((2, steps)),
    ]
    near = pl.BlockSpec(memory_space=pltpu.VMEM)
    far = pl.BlockSpec(memory_space=pl.ANY)
    return pl.pallas_call(
        functools.partial(whole_kernel, regions, members),
        out_shape=(
            jax.ShapeDtypeStruct((1, roots), jnp.float32),
            jax.ShapeDtypeStruct((1, knots // regions), jnp.float32),
            jax.ShapeDtypeStruct((slots // BLOCK, BLOCK), jnp.float32),
        ),
        in_specs=[near, near, far, far, near, near, near],
        out_specs=(near, near, near),
        scratch_shapes=scratch,
        compiler_params=pltpu.CompilerParams(
            collective_id=0, has_side_effects=True, vmem_limit_bytes=56 * 1024 * 1024
        ),
        name="posterior",
    )(
        observed.reshape(slots // BLOCK, BLOCK),
        noise.reshape(slots // BLOCK, BLOCK),
        mid_basis,
        root_basis,
        mid_prior,
        root_prior[None, :],
        leaf_count,
    )


def publish_kernel(*refs):
    for source, target in zip(refs[:3], refs[3:]):
        target[...] = source[...]


def on_device(observed, noise_precision, mid_basis, root_basis, mid_prior, root_prior, leaf_count):
    results = whole(
        observed, noise_precision, mid_basis, root_basis, mid_prior, root_prior, leaf_count
    )
    root_means, middle, leaf = pl.pallas_call(
        publish_kernel,
        out_shape=tuple(jax.ShapeDtypeStruct(x.shape, x.dtype) for x in results),
        name="publish",
    )(*results)
    return (root_means[0], middle, leaf.reshape(-1))


def solution(mesh):
    return jax.shard_map(
        on_device,
        mesh=mesh,
        in_specs=(
            P(("group", "region")),
            P(("group", "region")),
            P(("group", "region"), None),
            P(("group", "region"), None),
            P("group", None),
            P(),
            P("group", "region"),
        ),
        out_specs=(P(), P("group", "region"), P(("group", "region"))),
        check_vma=False,
    )
```

```python
import functools

import jax
import jax.numpy as jnp
from jax import lax
from jax.experimental import pallas as pl
from jax.experimental.pallas import tpu as pltpu
from jax.sharding import PartitionSpec as P

HIGHEST = lax.Precision.HIGHEST
MESH = pl.DeviceIdType.MESH
BLOCK = 128
PANEL = 8
WIDE = 16
LOADS = 4


def mxu(a, b):
    return jnp.dot(a, b, precision=HIGHEST, preferred_element_type=jnp.float32)


def mxu_tn(a, b):
    return lax.dot_general(
        a, b, (((0,), (0,)), ((), ())), precision=HIGHEST, preferred_element_type=jnp.float32
    )


def mxu_nt(a, b):
    return lax.dot_general(
        a, b, (((1,), (1,)), ((), ())), precision=HIGHEST, preferred_element_type=jnp.float32
    )


def split(x):
    high = x.astype(jnp.bfloat16)
    return high, (x - high.astype(jnp.float32)).astype(jnp.bfloat16)


def split3(x):
    high = x.astype(jnp.bfloat16)
    rest = x - high.astype(jnp.float32)
    mid = rest.astype(jnp.bfloat16)
    return high, mid, (rest - mid.astype(jnp.float32)).astype(jnp.bfloat16)


def bf(a, b):
    return jnp.dot(a, b, preferred_element_type=jnp.float32)


def beside(a, b):
    return jnp.concatenate([a, b], axis=1)


def above(a, b):
    return jnp.concatenate([a, b], axis=0)


def negated_inverse(groups, midway=None):
    count = len(groups)
    size = count * PANEL
    shape = (PANEL, size)
    per = WIDE // PANEL
    lane = lax.broadcasted_iota(jnp.int32, shape, 1)
    sub = lax.broadcasted_iota(jnp.int32, shape, 0)

    def row_of(value, k):
        return jnp.broadcast_to(value[k : k + 1, :], shape)

    def column_of(value, k):
        return jnp.broadcast_to(value[:, k : k + 1], shape)

    for p in range(size // WIDE):
        if midway is not None and p == size // WIDE // 2:
            midway()
        first = p * WIDE
        inside = (lane >= first) & (lane < first + WIDE)
        mine = groups[p * per : (p + 1) * per]
        cols = [[column_of(g, first + k) for g in mine] for k in range(WIDE)]
        work = [
            jnp.where(lane == first + PANEL * i + sub, -1.0, jnp.where(inside, 0.0, g))
            for i, g in enumerate(mine)
        ]
        for k in range(0, WIDE, 2):
            at, s = k // PANEL, k % PANEL
            left, right = cols[k], cols[k + 1]
            top, side, low = row_of(left[at], s), row_of(right[at], s), row_of(right[at], s + 1)
            inv = 1.0 / (top * low - side * side)
            inv_top, inv_side, inv_low = low * inv, -side * inv, top * inv
            former = [left[v] * inv_top + right[v] * inv_side for v in range(per)]
            latter = [left[v] * inv_side + right[v] * inv_low for v in range(per)]
            former[at] = jnp.where(sub == s, -inv_top, jnp.where(sub == s + 1, -inv_side, former[at]))
            latter[at] = jnp.where(sub == s, -inv_side, jnp.where(sub == s + 1, -inv_low, latter[at]))
            pivot = (sub == s) | (sub == s + 1)

            def cleared(target):
                upper, lower = row_of(target[at], s), row_of(target[at], s + 1)
                base = list(target)
                base[at] = jnp.where(pivot, 0.0, base[at])
                return [base[v] - former[v] * upper - latter[v] * lower for v in range(per)]

            for j in range(k + 2, WIDE):
                cols[j] = cleared(cols[j])
            work = cleared(work)
        near = [i for i in range((p + 1) * per, (p + 2) * per) if i < count]
        far = [i for i in range(count) if i // per != p and i not in near]
        after = list(groups)
        spread = [row_of(work[k // PANEL], k % PANEL) for k in range(WIDE)]
        for i in near:
            value = jnp.where(inside, 0.0, groups[i])
            for k in range(WIDE):
                value = value - column_of(groups[i], first + k) * spread[k]
            after[i] = value
        blank = jnp.zeros(shape, jnp.float32)
        padded = [work[i - p * per] if i // per == p else blank for i in range(count)]
        row_high, row_mid, row_low = split3(jnp.concatenate(padded, axis=0))
        high, mid, low = split3(jnp.concatenate(groups, axis=0))
        both = beside(high, mid)
        product = (
            bf(both, above(row_high, row_high))
            + bf(both, above(row_mid, row_mid))
            + bf(beside(low, high), above(row_high, row_low))
        )
        for i in far:
            after[i] = jnp.where(inside, 0.0, groups[i]) - product[i * PANEL : (i + 1) * PANEL, :]
        for i in range(per):
            after[p * per + i] = work[i]
        groups = after
    return groups


def each_block(a_ref, inv_ref, hooks, tails):
    blocks = a_ref.shape[0] // BLOCK

    def step(kb, carry):
        own = pl.ds(pl.multiple_of(kb * BLOCK, BLOCK), BLOCK)
        diagonal = a_ref[own, own]
        groups = [diagonal[i * PANEL : (i + 1) * PANEL, :] for i in range(BLOCK // PANEL)]

        def run(point):
            for (at, where), hook in hooks.items():
                if where == point:
                    pl.when(kb == at)(hook)

        inverse = -jnp.concatenate(negated_inverse(groups, functools.partial(run, 0)), axis=0)
        inv_ref[own, :] = inverse
        run(1)
        for at, tail in tails.items():
            pl.when(kb == at)(tail)
        return carry

    lax.fori_loop(0, blocks, step, 0)


def eliminate(a_ref, row_ref, inv_ref, k, first, last):
    if first >= last:
        return
    cols = slice(first * BLOCK, last * BLOCK)
    upper = a_ref[span(k), cols]
    row = mxu(inv_ref[span(k), :], upper)
    row_ref[span(k), cols] = row
    a_ref[cols, cols] = a_ref[cols, cols] - mxu_tn(upper, row)


def factor_tails(a_ref, row_ref, inv_ref, part, arrive):
    blocks = a_ref.shape[0] // BLOCK
    rest = slice(part * BLOCK, blocks * BLOCK)

    def lead_tail(k):
        eliminate(a_ref, row_ref, inv_ref, k, k + 1, part)

    def join():
        arrive()
        for k in range(part):
            upper = a_ref[span(k), rest]
            row = mxu(inv_ref[span(k), :], upper)
            row_ref[span(k), rest] = row
            if k + 1 < part:
                inner = slice((k + 1) * BLOCK, part * BLOCK)
                a_ref[inner, rest] = a_ref[inner, rest] - mxu_tn(a_ref[span(k), inner], row)
            a_ref[rest, rest] = a_ref[rest, rest] - mxu_tn(upper, row)

    def rest_tail(k):
        eliminate(a_ref, row_ref, inv_ref, k, k + 1, blocks)

    tails = {k: functools.partial(lead_tail, k) for k in range(part - 1)}
    tails[part - 1] = join
    for k in range(part, blocks - 1):
        tails[k] = functools.partial(rest_tail, k)
    return tails


def span(i):
    return slice(i * BLOCK, (i + 1) * BLOCK)


def block_pairs(first, last):
    return [(i, j) for i in range(first, last) for j in range(i + 1)]


def diagonal_of(prior_ref, i):
    rows = lax.broadcasted_iota(jnp.int32, (BLOCK, BLOCK), 0)
    cols = lax.broadcasted_iota(jnp.int32, (BLOCK, BLOCK), 1)
    return jnp.where(rows == cols, prior_ref[:, span(i)], 0.0)


def place_upper(matrix_ref, packed_ref, prior_ref, pairs):
    for t, (i, j) in enumerate(pairs):
        value = packed_ref[span(t), :]
        if i == j:
            matrix_ref[span(i), span(i)] = value + diagonal_of(prior_ref, i)
        else:
            turned = value.T
            matrix_ref[span(j), span(i)] = turned
            if symmetric_at(pairs, j):
                matrix_ref[span(i), span(j)] = value


def symmetric_at(pairs, j):
    return (j, j) in pairs


def fill(packed_ref, base, value):
    tail = packed_ref.shape[0] - base
    if tail:
        packed_ref[base:, :] = jnp.zeros((tail, BLOCK), jnp.float32)
    if value is not None:
        for i in range(value.shape[1] // BLOCK):
            packed_ref[base + i : base + i + 1, :] = value[0:1, span(i)]


def unpack_row(packed_ref, base, size):
    parts = [packed_ref[base + i : base + i + 1, :] for i in range(size // BLOCK)]
    return jnp.broadcast_to(jnp.concatenate(parts, axis=1), (PANEL, size))


class Exchange:
    def __init__(self, slot, refs, sems, order):
        self.me = lax.axis_index("region")
        self.regions = 1 << sum(bits for _, bits in order)
        self.levels = len(order)
        self.slot = slot
        self.total = refs[0]
        self.works = refs[1 : 1 + self.levels]
        self.lands = refs[1 + self.levels :]
        self.sems = sems
        self.buffer = self.works[0]
        self.counts = [1 << bits for _, bits in order]
        self.strides = [1 << first for first, _ in order]
        self.own, self.offsets, self.sizes = [], [0], [self.buffer.shape[0]]
        for count, stride in zip(self.counts, self.strides):
            own = (self.me // stride) % count
            self.own.append(own)
            self.sizes.append(self.sizes[-1] // count)
            self.offsets.append(self.offsets[-1] + own * self.sizes[-1])

    def part(self, level, index):
        size = self.sizes[level + 1]
        return pl.ds(pl.multiple_of(index * size, PANEL), size)

    def range_at(self, level):
        return pl.ds(pl.multiple_of(self.offsets[level], PANEL), self.sizes[level])

    def copy(self, which, level, d, device, source, target):
        send, recv = self.sems
        return pltpu.make_async_remote_copy(
            src_ref=source,
            dst_ref=target,
            send_sem=send.at[self.slot * 2 + which, level, d - 1],
            recv_sem=recv.at[self.slot * 2 + which, level, d - 1],
            device_id={"region": device},
            device_id_type=MESH,
        )

    def partner(self, level, d):
        index = (self.own[level] + d) % self.counts[level]
        return index, self.me + (index - self.own[level]) * self.strides[level]

    def reduce_copies(self, level):
        copies = []
        for d in range(1, self.counts[level]):
            index, device = self.partner(level, d)
            source = self.works[level].at[self.part(level, index)]
            copies.append(self.copy(0, level, d, device, source, self.lands[level].at[d - 1]))
        return copies

    def gather_copies(self, level):
        held = self.total.at[self.range_at(level + 1)]
        return [
            self.copy(1, level, d, self.partner(level, d)[1], held, held)
            for d in range(1, self.counts[level])
        ]

    def summed(self, level):
        wait_all(self.reduce_copies(level))
        value = self.works[level][self.part(level, self.own[level]), :]
        for d in range(1, self.counts[level]):
            value = value + self.lands[level][d - 1]
        return value

    def reduce(self, level):
        if level:
            self.works[level][...] = self.summed(level - 1)
        start_all(self.reduce_copies(level))

    def slab_sum(self):
        return self.summed(self.levels - 1)

    def slab_at(self):
        return self.range_at(self.levels)

    def start_gather(self, value=None):
        self.total[self.slab_at(), :] = self.slab_sum() if value is None else value
        start_all(self.gather_copies(self.levels - 1))

    def gather(self, level):
        wait_all(self.gather_copies(level + 1))
        start_all(self.gather_copies(level))

    def finish(self):
        wait_all(self.gather_copies(0))


def start_all(copies):
    for copy in copies:
        copy.start()


def wait_all(copies):
    for copy in copies:
        copy.wait()


def advance(piece, *levels):
    for level in levels:
        if level < piece.levels:
            piece.reduce(level)
        elif level == piece.levels:
            piece.start_gather()
        else:
            piece.gather(2 * piece.levels - 1 - level)


PIECES = 6


def whole_kernel(
    orders, members,
    observed_ref, noise_ref, mid_ref, root_ref, mid_prior_ref, root_prior_ref, count_ref,
    root_out, mid_out, leaf_out,
    *scratch,
):
    refs = list(scratch)
    pieces = [[refs.pop(0) for _ in range(1 + 2 * len(order))] for order in orders]
    levels = len(orders[2])
    regions = 1 << levels
    (
        basis_mid, basis_root, scale_col, value_col, scale_row, value_row,
        mid_high, mid_low, root_high, root_low,
        mid_t_high, mid_t_low, root_t_high, root_t_low,
        inverse_ref, inv_ref, row_ref, full_ref, solved_ref, schur_ref,
        work_lead, land_lead, work_rest, land_rest,
        load_sem, piece_send, piece_recv, group_send, group_recv,
    ) = refs
    slots, knots = basis_mid.shape
    roots = basis_root.shape[1]
    blocks, root_blocks = knots // BLOCK, roots // BLOCK
    part, root_part = blocks // 2, root_blocks // 2
    cut, root_cut = part * BLOCK, root_part * BLOCK
    me = lax.axis_index("region")
    group = lax.axis_index("group")
    steps = members.bit_length() - 1
    partners = []
    for s in range(steps):
        bit = 1 << s
        partners.append(group + bit * (1 - 2 * ((group // bit) % 2)))
    barrier = pltpu.get_barrier_semaphore()
    for partner in partners:
        pl.semaphore_signal(barrier, inc=1, device_id={"group": partner}, device_id_type=MESH)
    peers = [me + 1 - 2 * (me % 2)]
    for d in range(1, regions // 2):
        peers.append((me // 2 + d) % (regions // 2) * 2 + me % 2)
    for peer in peers:
        pl.semaphore_signal(barrier, inc=1, device_id={"region": peer}, device_id_type=MESH)
    sems = (piece_send, piece_recv)
    lead, rest, cross_lead, cross_rest, root_lead, root_rest = [
        Exchange(slot, pieces[slot], sems, orders[slot]) for slot in range(PIECES)
    ]

    load_rows = slots // LOADS

    def load(which, c):
        source, target = ((mid_ref, basis_mid), (root_ref, basis_root))[which]
        at = pl.ds(c * load_rows, load_rows)
        return pltpu.make_async_copy(source.at[at], target.at[at], load_sem.at[which, c])

    for c in range(LOADS):
        load(0, c).start()
    shape = noise_ref.shape
    index = lax.broadcasted_iota(jnp.int32, shape, 0) * BLOCK + lax.broadcasted_iota(
        jnp.int32, shape, 1
    )
    weight = jnp.where(index < count_ref[...], noise_ref[...], 0.0)
    scale = jnp.sqrt(weight)
    scale_row[...] = scale
    value_row[...] = scale * observed_ref[...]

    def spread(c, carry):
        at = pl.ds(pl.multiple_of(c * BLOCK, BLOCK), BLOCK)
        square = (BLOCK, BLOCK)
        scale_col[at, :] = jnp.broadcast_to(scale_row[pl.ds(c, 1), :], square).T
        value_col[at, :] = jnp.broadcast_to(value_row[pl.ds(c, 1), :], square).T
        return carry

    lax.fori_loop(0, slots // BLOCK, spread, 0)

    def scaled(which, basis, high_ref, low_ref, t_high_ref, t_low_ref):
        width = basis.shape[1]
        wide = width // BLOCK

        def chunk(c, total):
            at = pl.ds(pl.multiple_of(c * BLOCK, BLOCK), BLOCK)
            scales = scale_col[at, :]
            value = basis[at, :] * jnp.concatenate([scales] * wide, axis=1)
            high, low = split(value)
            high_ref[at, :] = high
            low_ref[at, :] = low
            t_high_ref[:, at] = high.T
            t_low_ref[:, at] = low.T
            values = value_col[at, :]
            term = value * jnp.concatenate([values] * wide, axis=1)
            for i in range(BLOCK // PANEL):
                total = total + term[i * PANEL : (i + 1) * PANEL, :]
            return total

        total = jnp.zeros((PANEL, width), jnp.float32)
        per = load_rows // BLOCK
        for c in range(LOADS):
            load(which, c).wait()
            if which == 0:
                load(1, c).start()
            total = lax.fori_loop(c * per, (c + 1) * per, chunk, total)
        return jnp.sum(total, axis=0, keepdims=True)

    def gram(left, right, rows, cols):
        left_high, left_low = left
        right_high, right_low = right
        return (
            bf(left_high[rows, :], right_high[:, cols])
            + bf(left_high[rows, :], right_low[:, cols])
            + bf(left_low[rows, :], right_high[:, cols])
        )

    def symmetric(left, right, rows):
        left_high, _ = left
        right_high, right_low = right
        near = bf(left_high[rows, :], right_low[:, rows])
        return bf(left_high[rows, :], right_high[:, rows]) + near + near.T

    def put(piece, pairs, rows, cols, value):
        for t, (i, j) in enumerate(pairs):
            if rows <= i < rows + value.shape[0] // BLOCK and cols <= j < cols + value.shape[1] // BLOCK:
                piece.buffer[span(t), :] = value[span(i - rows), span(j - cols)]

    lead_pairs, rest_pairs = block_pairs(0, part), block_pairs(part, blocks)
    root_lead_pairs = block_pairs(0, root_part)
    root_rest_pairs = block_pairs(root_part, root_blocks)
    mid_rhs = scaled(0, basis_mid, mid_high, mid_low, mid_t_high, mid_t_low)
    mid_left, mid_right = (mid_t_high, mid_t_low), (mid_high, mid_low)
    root_left, root_right = (root_t_high, root_t_low), (root_high, root_low)
    low_half, high_half = slice(0, cut), slice(cut, knots)
    root_low_half, root_high_half = slice(0, root_cut), slice(root_cut, roots)

    fill(lead.buffer, len(lead_pairs) * BLOCK, None)
    put(lead, lead_pairs, 0, 0, symmetric(mid_left, mid_right, low_half))
    pl.semaphore_wait(barrier, steps + regions // 2)
    advance(lead, 0)
    fill(rest.buffer, len(rest_pairs) * BLOCK, None)
    put(rest, rest_pairs, part, 0, gram(mid_left, mid_right, high_half, low_half))
    put(rest, rest_pairs, part, part, symmetric(mid_left, mid_right, high_half))
    advance(rest, 0)
    advance(lead, 1)
    root_rhs = scaled(1, basis_root, root_high, root_low, root_t_high, root_t_low)
    advance(lead, 2)

    def put_cross(piece, first, last):
        for half in (low_half, high_half):
            value = gram(mid_left, root_right, half, slice(first * BLOCK, last * BLOCK))
            for j in range(first, last):
                at = (j - first) * knots + half.start
                piece.buffer[at : at + cut, :] = value[:, span(j - first)]

    fill(cross_lead.buffer, root_part * knots, None)
    put_cross(cross_lead, 0, root_part)
    advance(cross_lead, 0)
    advance(rest, 1)
    cross_base = (root_blocks - root_part) * knots
    fill(cross_rest.buffer, cross_base, mid_rhs)
    put_cross(cross_rest, root_part, root_blocks)
    advance(lead, 3)
    advance(cross_rest, 0)
    fill(root_lead.buffer, len(root_lead_pairs) * BLOCK, None)
    put(root_lead, root_lead_pairs, 0, 0, symmetric(root_left, root_right, root_low_half))
    root_base = len(root_rest_pairs) * BLOCK
    fill(root_rest.buffer, root_base, root_rhs)
    put(
        root_rest, root_rest_pairs, root_part, 0,
        gram(root_left, root_right, root_high_half, root_low_half),
    )
    put(
        root_rest, root_rest_pairs, root_part, root_part,
        symmetric(root_left, root_right, root_high_half),
    )
    advance(rest, 2)
    advance(cross_lead, *range(1, levels - 1))
    lead.finish()
    place_upper(inverse_ref, lead.total, mid_prior_ref, lead_pairs)

    def mid_arrive():
        rest.finish()
        place_upper(inverse_ref, rest.total, mid_prior_ref, rest_pairs)

    inner = range(1, levels - 1)
    outer = range(levels + 1, 2 * levels - 1)

    def stage(*moves):
        def run():
            for piece, *at in moves:
                advance(piece, *at)

        return run

    last = blocks - 1
    hooks = {
        (0, 0): stage((cross_lead, levels - 1)),
        (0, 1): stage((rest, 3), (cross_rest, *inner), (root_lead, 0), (root_rest, 0)),
        (1, 0): stage((cross_lead, levels), (cross_rest, levels - 1)),
        (1, 1): stage((cross_lead, *outer)),
        (last - 1, 0): stage((cross_rest, levels), (cross_lead, 2 * levels - 1)),
        (last - 1, 1): stage((root_lead, 1), (cross_rest, *outer)),
        (last, 0): stage((root_rest, 1), (cross_rest, 2 * levels - 1)),
    }
    each_block(
        inverse_ref, inv_ref, hooks,
        factor_tails(inverse_ref, row_ref, inv_ref, part, mid_arrive),
    )
    own_lead = root_lead.slab_sum()
    own_rest = root_rest.slab_sum()
    cross_lead.finish()
    for j in range(root_part):
        full_ref[:, span(j)] = cross_lead.total[j * knots : (j + 1) * knots, :]
    cross_rest.finish()
    for j in range(root_part, root_blocks):
        at = (j - root_part) * knots
        full_ref[:, span(j)] = cross_rest.total[at : at + knots, :]
    rhs_row = unpack_row(cross_rest.total, cross_base, knots)
    remaining = [rhs_row[:, span(k)] for k in range(blocks)]
    solved_parts = []
    for k in range(blocks):
        later = slice((k + 1) * BLOCK, knots)
        own_rows = full_ref[span(k), :]
        if k + 1 < blocks:
            row = row_ref[span(k), later]
            full_ref[later, :] = full_ref[later, :] - mxu_tn(row, own_rows)
            change = mxu(remaining[k], row)
            for i in range(k + 1, blocks):
                remaining[i] = remaining[i] - change[:, span(i - k - 1)]
        solved_ref[span(k), :] = mxu(inv_ref[span(k), :], own_rows)
        solved_parts.append(mxu(remaining[k], inv_ref[span(k), :]))

    def schur(piece, pairs):
        for t, (i, j) in enumerate(pairs):
            if j == 0:
                rows = mxu_tn(full_ref[:, span(i)], solved_ref[:, : (i + 1) * BLOCK])
            schur_ref[span(t), :] = rows[:, span(j)]

    def combine(s, work, land, semaphore):
        return pltpu.make_async_remote_copy(
            src_ref=work.at[s],
            dst_ref=land.at[s],
            send_sem=group_send.at[semaphore, s],
            recv_sem=group_recv.at[semaphore, s],
            device_id={"group": partners[s]},
            device_id_type=MESH,
        )

    schur(root_lead, root_lead_pairs)
    fill(schur_ref, len(root_lead_pairs) * BLOCK, None)
    work_lead[0] = own_lead - schur_ref[root_lead.slab_at(), :]
    combine(0, work_lead, land_lead, 0).start()
    schur(root_rest, root_rest_pairs)
    fill(schur_ref, root_base, mxu(jnp.concatenate(solved_parts, axis=1), full_ref[...]))
    work_rest[0] = own_rest - schur_ref[root_rest.slab_at(), :]
    combine(0, work_rest, land_rest, 1).start()
    for s in range(steps):
        for work, land, semaphore, piece in (
            (work_lead, land_lead, 0, root_lead),
            (work_rest, land_rest, 1, root_rest),
        ):
            combine(s, work, land, semaphore).wait()
            value = work[s] + land[s]
            if s + 1 < steps:
                work[s + 1] = value
                combine(s + 1, work, land, semaphore).start()
            else:
                piece.start_gather(value)
    advance(root_lead, 3)
    for k in reversed(range(blocks - 1)):
        later = slice((k + 1) * BLOCK, knots)
        row = row_ref[span(k), later]
        solved_ref[span(k), :] = solved_ref[span(k), :] - mxu(row, solved_ref[later, :])
        solved_parts[k] = solved_parts[k] - mxu_nt(
            jnp.concatenate(solved_parts[k + 1 :], axis=1), row
        )
    solved_rhs = jnp.concatenate(solved_parts, axis=1)
    advance(root_rest, 3)
    root_lead.finish()
    place_upper(inverse_ref, root_lead.total, root_prior_ref, root_lead_pairs)

    def root_arrive():
        root_rest.finish()
        place_upper(inverse_ref, root_rest.total, root_prior_ref, root_rest_pairs)

    each_block(
        inverse_ref, inv_ref, {},
        factor_tails(inverse_ref, row_ref, inv_ref, root_part, root_arrive),
    )
    vector = unpack_row(root_rest.total, root_base, roots)
    remaining = [vector[:, span(k)] for k in range(root_blocks)]
    weight_parts = []
    for k in range(root_blocks):
        if k + 1 < root_blocks:
            change = mxu(remaining[k], row_ref[span(k), (k + 1) * BLOCK : roots])
            for i in range(k + 1, root_blocks):
                remaining[i] = remaining[i] - change[:, span(i - k - 1)]
        weight_parts.append(mxu(remaining[k], inv_ref[span(k), :]))
    for k in reversed(range(root_blocks - 1)):
        weight_parts[k] = weight_parts[k] - mxu_nt(
            jnp.concatenate(weight_parts[k + 1 :], axis=1), row_ref[span(k), (k + 1) * BLOCK : roots]
        )
    weights = jnp.concatenate(weight_parts, axis=1)
    middle = solved_rhs - mxu_nt(weights, solved_ref[...])
    root_out[...] = weights[0:1, :]
    slab = mid_out.shape[1]
    turned = pltpu.roll(middle, (knots - me * slab) % knots, 1)
    mid_out[...] = turned[0:1, :slab]
    mid_rows = [jnp.broadcast_to(middle[0:1, span(j)], (BLOCK, BLOCK)) for j in range(blocks)]
    root_rows = [jnp.broadcast_to(weights[0:1, span(j)], (BLOCK, BLOCK)) for j in range(root_blocks)]

    for c in range(slots // BLOCK):
        at = span(c)
        total = jnp.zeros((BLOCK, BLOCK), jnp.float32)
        for j in range(blocks):
            total = total + basis_mid[at, span(j)] * mid_rows[j]
        for j in range(root_blocks):
            total = total + basis_root[at, span(j)] * root_rows[j]
        leaf_out[c : c + 1, :] = jnp.sum(total.T, axis=0, keepdims=True)


def round_up(value, unit):
    return (value + unit - 1) // unit * unit


def whole(observed, noise, mid_basis, root_basis, mid_prior, root_prior, leaf_count):
    slots, knots = mid_basis.shape
    roots = root_basis.shape[1]
    regions = lax.axis_size("region")
    members = lax.axis_size("group")
    steps = members.bit_length() - 1
    bits = regions.bit_length() - 1
    halving = tuple((bit, 1) for bit in range(bits))
    paired = ((0, 1), (1, bits - 1))
    orders = (paired, paired, halving, halving, paired, paired)
    unit = PANEL * regions
    blocks, root_blocks = knots // BLOCK, roots // BLOCK
    part, root_part = blocks // 2, root_blocks // 2
    sizes = [
        len(block_pairs(0, part)) * BLOCK,
        len(block_pairs(part, blocks)) * BLOCK,
        root_part * knots,
        (root_blocks - root_part) * knots + blocks,
        len(block_pairs(0, root_part)) * BLOCK,
        len(block_pairs(root_part, root_blocks)) * BLOCK + root_blocks,
    ]
    sizes = [round_up(size, unit) for size in sizes]

    def vmem(*shape):
        return pltpu.VMEM(shape, jnp.float32)

    def half(*shape):
        return pltpu.VMEM(shape, jnp.bfloat16)

    scratch = []
    for rows, order in zip(sizes, orders):
        counts = [1 << width for _, width in order]
        cuts = [rows]
        for count in counts:
            cuts.append(cuts[-1] // count)
        scratch.append(vmem(rows, BLOCK))
        scratch += [vmem(cut, BLOCK) for cut in cuts[:-1]]
        scratch += [vmem(count - 1, cut, BLOCK) for count, cut in zip(counts, cuts[1:])]
    scratch += [
        vmem(slots, knots),
        vmem(slots, roots),
        vmem(slots, BLOCK),
        vmem(slots, BLOCK),
        vmem(slots // BLOCK, BLOCK),
        vmem(slots // BLOCK, BLOCK),
        half(slots, knots),
        half(slots, knots),
        half(slots, roots),
        half(slots, roots),
        half(knots, slots),
        half(knots, slots),
        half(roots, slots),
        half(roots, slots),
        vmem(knots, knots),
        vmem(max(knots, roots), BLOCK),
        vmem(max(knots, roots), max(knots, roots)),
        vmem(knots, roots),
        vmem(knots, roots),
        vmem(max(sizes[4:]), BLOCK),
        vmem(steps, sizes[4] // regions, BLOCK),
        vmem(steps, sizes[4] // regions, BLOCK),
        vmem(steps, sizes[5] // regions, BLOCK),
        vmem(steps, sizes[5] // regions, BLOCK),
        pltpu.SemaphoreType.DMA((2, LOADS)),
        pltpu.SemaphoreType.DMA((2 * PIECES, bits, regions - 1)),
        pltpu.SemaphoreType.DMA((2 * PIECES, bits, regions - 1)),
        pltpu.SemaphoreType.DMA((2, steps)),
        pltpu.SemaphoreType.DMA((2, steps)),
    ]
    near = pl.BlockSpec(memory_space=pltpu.VMEM)
    far = pl.BlockSpec(memory_space=pl.ANY)
    return pl.pallas_call(
        functools.partial(whole_kernel, orders, members),
        out_shape=(
            jax.ShapeDtypeStruct((1, roots), jnp.float32),
            jax.ShapeDtypeStruct((1, knots // regions), jnp.float32),
            jax.ShapeDtypeStruct((slots // BLOCK, BLOCK), jnp.float32),
        ),
        in_specs=[near, near, far, far, near, near, near],
        out_specs=(near, near, near),
        scratch_shapes=scratch,
        compiler_params=pltpu.CompilerParams(
            collective_id=0, has_side_effects=True, vmem_limit_bytes=56 * 1024 * 1024
        ),
        name="posterior",
    )(
        observed.reshape(slots // BLOCK, BLOCK),
        noise.reshape(slots // BLOCK, BLOCK),
        mid_basis,
        root_basis,
        mid_prior,
        root_prior[None, :],
        leaf_count,
    )


def publish_kernel(*refs):
    for source, target in zip(refs[:3], refs[3:]):
        target[...] = source[...]


def on_device(observed, noise_precision, mid_basis, root_basis, mid_prior, root_prior, leaf_count):
    results = whole(
        observed, noise_precision, mid_basis, root_basis, mid_prior, root_prior, leaf_count
    )
    root_means, middle, leaf = pl.pallas_call(
        publish_kernel,
        out_shape=tuple(jax.ShapeDtypeStruct(x.shape, x.dtype) for x in results),
        name="publish",
    )(*results)
    return (root_means[0], middle, leaf.reshape(-1))


def solution(mesh):
    return jax.shard_map(
        on_device,
        mesh=mesh,
        in_specs=(
            P(("group", "region")),
            P(("group", "region")),
            P(("group", "region"), None),
            P(("group", "region"), None),
            P("group", None),
            P(),
            P("group", "region"),
        ),
        out_specs=(P(), P("group", "region"), P(("group", "region"))),
        check_vma=False,
    )
```

```python
import functools

import jax
import jax.numpy as jnp
from jax import lax
from jax.experimental import pallas as pl
from jax.experimental.pallas import tpu as pltpu
from jax.sharding import PartitionSpec as P

HIGHEST = lax.Precision.HIGHEST
MESH = pl.DeviceIdType.MESH
BLOCK = 128
PANEL = 8
WIDE = 16
LOADS = 4


def mxu(a, b):
    return jnp.dot(a, b, precision=HIGHEST, preferred_element_type=jnp.float32)


def mxu_tn(a, b):
    return lax.dot_general(
        a, b, (((0,), (0,)), ((), ())), precision=HIGHEST, preferred_element_type=jnp.float32
    )


def mxu_nt(a, b):
    return lax.dot_general(
        a, b, (((1,), (1,)), ((), ())), precision=HIGHEST, preferred_element_type=jnp.float32
    )


def split(x):
    high = x.astype(jnp.bfloat16)
    return high, (x - high.astype(jnp.float32)).astype(jnp.bfloat16)


def split3(x):
    high = x.astype(jnp.bfloat16)
    rest = x - high.astype(jnp.float32)
    mid = rest.astype(jnp.bfloat16)
    return high, mid, (rest - mid.astype(jnp.float32)).astype(jnp.bfloat16)


def bf(a, b):
    return jnp.dot(a, b, preferred_element_type=jnp.float32)


def beside(a, b):
    return jnp.concatenate([a, b], axis=1)


def above(a, b):
    return jnp.concatenate([a, b], axis=0)


def negated_inverse(groups, midway=None):
    count = len(groups)
    size = count * PANEL
    shape = (PANEL, size)
    per = WIDE // PANEL
    lane = lax.broadcasted_iota(jnp.int32, shape, 1)
    sub = lax.broadcasted_iota(jnp.int32, shape, 0)

    def row_of(value, k):
        return jnp.broadcast_to(value[k : k + 1, :], shape)

    def column_of(value, k):
        return jnp.broadcast_to(value[:, k : k + 1], shape)

    for p in range(size // WIDE):
        if midway is not None and p == size // WIDE // 2:
            midway()
        first = p * WIDE
        inside = (lane >= first) & (lane < first + WIDE)
        mine = groups[p * per : (p + 1) * per]
        cols = [[column_of(g, first + k) for g in mine] for k in range(WIDE)]
        work = [
            jnp.where(lane == first + PANEL * i + sub, -1.0, jnp.where(inside, 0.0, g))
            for i, g in enumerate(mine)
        ]
        for k in range(0, WIDE, 2):
            at, s = k // PANEL, k % PANEL
            left, right = cols[k], cols[k + 1]
            top, side, low = row_of(left[at], s), row_of(right[at], s), row_of(right[at], s + 1)
            inv = 1.0 / (top * low - side * side)
            inv_top, inv_side, inv_low = low * inv, -side * inv, top * inv
            former = [left[v] * inv_top + right[v] * inv_side for v in range(per)]
            latter = [left[v] * inv_side + right[v] * inv_low for v in range(per)]
            former[at] = jnp.where(sub == s, -inv_top, jnp.where(sub == s + 1, -inv_side, former[at]))
            latter[at] = jnp.where(sub == s, -inv_side, jnp.where(sub == s + 1, -inv_low, latter[at]))
            pivot = (sub == s) | (sub == s + 1)

            def cleared(target):
                upper, lower = row_of(target[at], s), row_of(target[at], s + 1)
                base = list(target)
                base[at] = jnp.where(pivot, 0.0, base[at])
                return [base[v] - former[v] * upper - latter[v] * lower for v in range(per)]

            for j in range(k + 2, WIDE):
                cols[j] = cleared(cols[j])
            work = cleared(work)
        near = [i for i in range((p + 1) * per, (p + 2) * per) if i < count]
        far = [i for i in range(count) if i // per != p and i not in near]
        after = list(groups)
        spread = [row_of(work[k // PANEL], k % PANEL) for k in range(WIDE)]
        for i in near:
            value = jnp.where(inside, 0.0, groups[i])
            for k in range(WIDE):
                value = value - column_of(groups[i], first + k) * spread[k]
            after[i] = value
        blank = jnp.zeros(shape, jnp.float32)
        padded = [work[i - p * per] if i // per == p else blank for i in range(count)]
        row_high, row_mid, row_low = split3(jnp.concatenate(padded, axis=0))
        high, mid, low = split3(jnp.concatenate(groups, axis=0))
        both = beside(high, mid)
        product = (
            bf(both, above(row_high, row_high))
            + bf(both, above(row_mid, row_mid))
            + bf(beside(low, high), above(row_high, row_low))
        )
        for i in far:
            after[i] = jnp.where(inside, 0.0, groups[i]) - product[i * PANEL : (i + 1) * PANEL, :]
        for i in range(per):
            after[p * per + i] = work[i]
        groups = after
    return groups


def each_block(a_ref, inv_ref, hooks, tails):
    blocks = a_ref.shape[0] // BLOCK

    def step(kb, carry):
        own = pl.ds(pl.multiple_of(kb * BLOCK, BLOCK), BLOCK)
        diagonal = a_ref[own, own]
        groups = [diagonal[i * PANEL : (i + 1) * PANEL, :] for i in range(BLOCK // PANEL)]

        def run(point):
            for (at, where), hook in hooks.items():
                if where == point:
                    pl.when(kb == at)(hook)

        inverse = -jnp.concatenate(negated_inverse(groups, functools.partial(run, 0)), axis=0)
        inv_ref[own, :] = inverse
        run(1)
        for at, tail in tails.items():
            pl.when(kb == at)(tail)
        return carry

    lax.fori_loop(0, blocks, step, 0)


def eliminate(a_ref, row_ref, inv_ref, k, first, last):
    if first >= last:
        return
    cols = slice(first * BLOCK, last * BLOCK)
    upper = a_ref[span(k), cols]
    row = mxu(inv_ref[span(k), :], upper)
    row_ref[span(k), cols] = row
    a_ref[cols, cols] = a_ref[cols, cols] - mxu_tn(upper, row)


def factor_tails(a_ref, row_ref, inv_ref, part, arrive):
    blocks = a_ref.shape[0] // BLOCK
    rest = slice(part * BLOCK, blocks * BLOCK)

    def lead_tail(k):
        eliminate(a_ref, row_ref, inv_ref, k, k + 1, part)

    def join():
        arrive()
        for k in range(part):
            upper = a_ref[span(k), rest]
            row = mxu(inv_ref[span(k), :], upper)
            row_ref[span(k), rest] = row
            if k + 1 < part:
                inner = slice((k + 1) * BLOCK, part * BLOCK)
                a_ref[inner, rest] = a_ref[inner, rest] - mxu_tn(a_ref[span(k), inner], row)
            a_ref[rest, rest] = a_ref[rest, rest] - mxu_tn(upper, row)

    def rest_tail(k):
        eliminate(a_ref, row_ref, inv_ref, k, k + 1, blocks)

    tails = {k: functools.partial(lead_tail, k) for k in range(part - 1)}
    tails[part - 1] = join
    for k in range(part, blocks - 1):
        tails[k] = functools.partial(rest_tail, k)
    return tails


def span(i):
    return slice(i * BLOCK, (i + 1) * BLOCK)


def block_pairs(first, last):
    return [(i, j) for i in range(first, last) for j in range(i + 1)]


def diagonal_of(prior_ref, i):
    rows = lax.broadcasted_iota(jnp.int32, (BLOCK, BLOCK), 0)
    cols = lax.broadcasted_iota(jnp.int32, (BLOCK, BLOCK), 1)
    return jnp.where(rows == cols, prior_ref[:, span(i)], 0.0)


def place_upper(matrix_ref, packed_ref, prior_ref, pairs):
    for t, (i, j) in enumerate(pairs):
        value = packed_ref[span(t), :]
        if i == j:
            matrix_ref[span(i), span(i)] = value + diagonal_of(prior_ref, i)
        else:
            turned = value.T
            matrix_ref[span(j), span(i)] = turned
            if symmetric_at(pairs, j):
                matrix_ref[span(i), span(j)] = value


def symmetric_at(pairs, j):
    return (j, j) in pairs


def fill(packed_ref, base, value):
    tail = packed_ref.shape[0] - base
    if tail:
        packed_ref[base:, :] = jnp.zeros((tail, BLOCK), jnp.float32)
    if value is not None:
        for i in range(value.shape[1] // BLOCK):
            packed_ref[base + i : base + i + 1, :] = value[0:1, span(i)]


def unpack_row(packed_ref, base, size):
    parts = [packed_ref[base + i : base + i + 1, :] for i in range(size // BLOCK)]
    return jnp.broadcast_to(jnp.concatenate(parts, axis=1), (PANEL, size))


class Exchange:
    def __init__(self, slot, refs, sems, order):
        self.me = lax.axis_index("region")
        self.regions = 1 << sum(bits for _, bits in order)
        self.levels = len(order)
        self.slot = slot
        self.total = refs[0]
        self.works = refs[1 : 1 + self.levels]
        self.lands = refs[1 + self.levels :]
        self.sems = sems
        self.buffer = self.works[0]
        self.counts = [1 << bits for _, bits in order]
        self.strides = [1 << first for first, _ in order]
        self.own, self.offsets, self.sizes = [], [0], [self.buffer.shape[0]]
        for count, stride in zip(self.counts, self.strides):
            own = (self.me // stride) % count
            self.own.append(own)
            self.sizes.append(self.sizes[-1] // count)
            self.offsets.append(self.offsets[-1] + own * self.sizes[-1])

    def part(self, level, index):
        size = self.sizes[level + 1]
        return pl.ds(pl.multiple_of(index * size, PANEL), size)

    def range_at(self, level):
        return pl.ds(pl.multiple_of(self.offsets[level], PANEL), self.sizes[level])

    def copy(self, which, level, d, device, source, target):
        send, recv = self.sems
        return pltpu.make_async_remote_copy(
            src_ref=source,
            dst_ref=target,
            send_sem=send.at[self.slot * 2 + which, level, d - 1],
            recv_sem=recv.at[self.slot * 2 + which, level, d - 1],
            device_id={"region": device},
            device_id_type=MESH,
        )

    def partner(self, level, d):
        index = (self.own[level] + d) % self.counts[level]
        return index, self.me + (index - self.own[level]) * self.strides[level]

    def reduce_copies(self, level):
        copies = []
        for d in range(1, self.counts[level]):
            index, device = self.partner(level, d)
            source = self.works[level].at[self.part(level, index)]
            copies.append(self.copy(0, level, d, device, source, self.lands[level].at[d - 1]))
        return copies

    def gather_copies(self, level):
        held = self.total.at[self.range_at(level + 1)]
        return [
            self.copy(1, level, d, self.partner(level, d)[1], held, held)
            for d in range(1, self.counts[level])
        ]

    def summed(self, level):
        wait_all(self.reduce_copies(level))
        value = self.works[level][self.part(level, self.own[level]), :]
        for d in range(1, self.counts[level]):
            value = value + self.lands[level][d - 1]
        return value

    def reduce(self, level):
        if level:
            self.works[level][...] = self.summed(level - 1)
        start_all(self.reduce_copies(level))

    def slab_sum(self):
        return self.summed(self.levels - 1)

    def slab_at(self):
        return self.range_at(self.levels)

    def start_gather(self, value=None):
        self.total[self.slab_at(), :] = self.slab_sum() if value is None else value
        start_all(self.gather_copies(self.levels - 1))

    def gather(self, level):
        wait_all(self.gather_copies(level + 1))
        start_all(self.gather_copies(level))

    def finish(self):
        wait_all(self.gather_copies(0))


def start_all(copies):
    for copy in copies:
        copy.start()


def wait_all(copies):
    for copy in copies:
        copy.wait()


def advance(piece, *levels):
    for level in levels:
        if level < piece.levels:
            piece.reduce(level)
        elif level == piece.levels:
            piece.start_gather()
        else:
            piece.gather(2 * piece.levels - 1 - level)


PIECES = 6


def whole_kernel(
    orders, members,
    observed_ref, noise_ref, mid_ref, root_ref, mid_prior_ref, root_prior_ref, count_ref,
    root_out, mid_out, leaf_out,
    *scratch,
):
    refs = list(scratch)
    pieces = [[refs.pop(0) for _ in range(1 + 2 * len(order))] for order in orders]
    levels = len(orders[2])
    regions = 1 << levels
    (
        basis_mid, basis_root, scale_col, value_col, scale_row, value_row,
        mid_high, mid_low, root_high, root_low,
        mid_t_high, mid_t_low, root_t_high, root_t_low,
        inverse_ref, inv_ref, row_ref, full_ref, solved_ref, schur_ref, vector_ref, found_ref,
        work_lead, land_lead, work_rest, land_rest,
        load_sem, piece_send, piece_recv, group_send, group_recv,
    ) = refs
    slots, knots = basis_mid.shape
    roots = basis_root.shape[1]
    blocks, root_blocks = knots // BLOCK, roots // BLOCK
    part, root_part = blocks // 2, root_blocks // 2
    cut, root_cut = part * BLOCK, root_part * BLOCK
    me = lax.axis_index("region")
    group = lax.axis_index("group")
    steps = members.bit_length() - 1
    partners = []
    for s in range(steps):
        bit = 1 << s
        partners.append(group + bit * (1 - 2 * ((group // bit) % 2)))
    barrier = pltpu.get_barrier_semaphore()
    for partner in partners:
        pl.semaphore_signal(barrier, inc=1, device_id={"group": partner}, device_id_type=MESH)
    peers = [me + 1 - 2 * (me % 2)]
    for d in range(1, regions // 2):
        peers.append((me // 2 + d) % (regions // 2) * 2 + me % 2)
    for peer in peers:
        pl.semaphore_signal(barrier, inc=1, device_id={"region": peer}, device_id_type=MESH)
    sems = (piece_send, piece_recv)
    lead, rest, cross_lead, cross_rest, root_lead, root_rest = [
        Exchange(slot, pieces[slot], sems, orders[slot]) for slot in range(PIECES)
    ]

    load_rows = slots // LOADS

    def load(which, c):
        source, target = ((mid_ref, basis_mid), (root_ref, basis_root))[which]
        at = pl.ds(c * load_rows, load_rows)
        return pltpu.make_async_copy(source.at[at], target.at[at], load_sem.at[which, c])

    for c in range(LOADS):
        load(0, c).start()
    shape = noise_ref.shape
    index = lax.broadcasted_iota(jnp.int32, shape, 0) * BLOCK + lax.broadcasted_iota(
        jnp.int32, shape, 1
    )
    weight = jnp.where(index < count_ref[...], noise_ref[...], 0.0)
    scale = jnp.sqrt(weight)
    scale_row[...] = scale
    value_row[...] = scale * observed_ref[...]

    def spread(c, carry):
        at = pl.ds(pl.multiple_of(c * BLOCK, BLOCK), BLOCK)
        square = (BLOCK, BLOCK)
        scale_col[at, :] = jnp.broadcast_to(scale_row[pl.ds(c, 1), :], square).T
        value_col[at, :] = jnp.broadcast_to(value_row[pl.ds(c, 1), :], square).T
        return carry

    lax.fori_loop(0, slots // BLOCK, spread, 0)

    def scaled(which, basis, high_ref, low_ref, t_high_ref, t_low_ref):
        width = basis.shape[1]
        wide = width // BLOCK

        def chunk(c, total):
            at = pl.ds(pl.multiple_of(c * BLOCK, BLOCK), BLOCK)
            scales = scale_col[at, :]
            value = basis[at, :] * jnp.concatenate([scales] * wide, axis=1)
            high, low = split(value)
            high_ref[at, :] = high
            low_ref[at, :] = low
            t_high_ref[:, at] = high.T
            t_low_ref[:, at] = low.T
            values = value_col[at, :]
            term = value * jnp.concatenate([values] * wide, axis=1)
            for i in range(BLOCK // PANEL):
                total = total + term[i * PANEL : (i + 1) * PANEL, :]
            return total

        total = jnp.zeros((PANEL, width), jnp.float32)
        per = load_rows // BLOCK
        for c in range(LOADS):
            load(which, c).wait()
            if which == 0:
                load(1, c).start()
            total = lax.fori_loop(c * per, (c + 1) * per, chunk, total)
        return jnp.sum(total, axis=0, keepdims=True)

    def gram(left, right, rows, cols):
        left_high, left_low = left
        right_high, right_low = right
        return (
            bf(left_high[rows, :], right_high[:, cols])
            + bf(left_high[rows, :], right_low[:, cols])
            + bf(left_low[rows, :], right_high[:, cols])
        )

    def symmetric(left, right, rows):
        left_high, _ = left
        right_high, right_low = right
        near = bf(left_high[rows, :], right_low[:, rows])
        return bf(left_high[rows, :], right_high[:, rows]) + near + near.T

    def put(piece, pairs, rows, cols, value):
        for t, (i, j) in enumerate(pairs):
            if rows <= i < rows + value.shape[0] // BLOCK and cols <= j < cols + value.shape[1] // BLOCK:
                piece.buffer[span(t), :] = value[span(i - rows), span(j - cols)]

    lead_pairs, rest_pairs = block_pairs(0, part), block_pairs(part, blocks)
    root_lead_pairs = block_pairs(0, root_part)
    root_rest_pairs = block_pairs(root_part, root_blocks)
    mid_rhs = scaled(0, basis_mid, mid_high, mid_low, mid_t_high, mid_t_low)
    mid_left, mid_right = (mid_t_high, mid_t_low), (mid_high, mid_low)
    root_left, root_right = (root_t_high, root_t_low), (root_high, root_low)
    low_half, high_half = slice(0, cut), slice(cut, knots)
    root_low_half, root_high_half = slice(0, root_cut), slice(root_cut, roots)

    fill(lead.buffer, len(lead_pairs) * BLOCK, None)
    put(lead, lead_pairs, 0, 0, symmetric(mid_left, mid_right, low_half))
    pl.semaphore_wait(barrier, steps + regions // 2)
    advance(lead, 0)
    fill(rest.buffer, len(rest_pairs) * BLOCK, None)
    put(rest, rest_pairs, part, 0, gram(mid_left, mid_right, high_half, low_half))
    put(rest, rest_pairs, part, part, symmetric(mid_left, mid_right, high_half))
    advance(rest, 0)
    advance(lead, 1)
    root_rhs = scaled(1, basis_root, root_high, root_low, root_t_high, root_t_low)
    advance(lead, 2)

    def put_cross(piece, first, last):
        for half in (low_half, high_half):
            value = gram(mid_left, root_right, half, slice(first * BLOCK, last * BLOCK))
            for j in range(first, last):
                at = (j - first) * knots + half.start
                piece.buffer[at : at + cut, :] = value[:, span(j - first)]

    fill(cross_lead.buffer, root_part * knots, None)
    put_cross(cross_lead, 0, root_part)
    advance(cross_lead, 0)
    advance(rest, 1)
    cross_base = (root_blocks - root_part) * knots
    fill(cross_rest.buffer, cross_base, mid_rhs)
    put_cross(cross_rest, root_part, root_blocks)
    advance(lead, 3)
    advance(cross_rest, 0)
    fill(root_lead.buffer, len(root_lead_pairs) * BLOCK, None)
    put(root_lead, root_lead_pairs, 0, 0, symmetric(root_left, root_right, root_low_half))
    root_base = len(root_rest_pairs) * BLOCK
    fill(root_rest.buffer, root_base, root_rhs)
    put(
        root_rest, root_rest_pairs, root_part, 0,
        gram(root_left, root_right, root_high_half, root_low_half),
    )
    put(
        root_rest, root_rest_pairs, root_part, root_part,
        symmetric(root_left, root_right, root_high_half),
    )
    advance(rest, 2)
    advance(cross_lead, *range(1, levels - 1))
    lead.finish()
    place_upper(inverse_ref, lead.total, mid_prior_ref, lead_pairs)

    def mid_arrive():
        rest.finish()
        place_upper(inverse_ref, rest.total, mid_prior_ref, rest_pairs)

    inner = range(1, levels - 1)
    outer = range(levels + 1, 2 * levels - 1)

    def stage(*moves):
        def run():
            for piece, *at in moves:
                advance(piece, *at)

        return run

    last = blocks - 1
    hooks = {
        (0, 0): stage((cross_lead, levels - 1)),
        (0, 1): stage((rest, 3), (cross_rest, *inner), (root_lead, 0), (root_rest, 0)),
        (1, 0): stage((cross_lead, levels), (cross_rest, levels - 1)),
        (1, 1): stage((cross_lead, *outer)),
        (last - 1, 0): stage((cross_rest, levels), (cross_lead, 2 * levels - 1)),
        (last - 1, 1): stage((root_lead, 1), (cross_rest, *outer)),
        (last, 0): stage((root_rest, 1), (cross_rest, 2 * levels - 1)),
    }
    each_block(
        inverse_ref, inv_ref, hooks,
        factor_tails(inverse_ref, row_ref, inv_ref, part, mid_arrive),
    )
    own_lead = root_lead.slab_sum()
    own_rest = root_rest.slab_sum()
    cross_lead.finish()
    for j in range(root_part):
        full_ref[:, span(j)] = cross_lead.total[j * knots : (j + 1) * knots, :]
    cross_rest.finish()
    for j in range(root_part, root_blocks):
        at = (j - root_part) * knots
        full_ref[:, span(j)] = cross_rest.total[at : at + knots, :]
    rhs_row = unpack_row(cross_rest.total, cross_base, knots)
    remaining = [rhs_row[:, span(k)] for k in range(blocks)]
    solved_parts = []
    for k in range(blocks):
        later = slice((k + 1) * BLOCK, knots)
        own_rows = full_ref[span(k), :]
        if k + 1 < blocks:
            row = row_ref[span(k), later]
            full_ref[later, :] = full_ref[later, :] - mxu_tn(row, own_rows)
            change = mxu(remaining[k], row)
            for i in range(k + 1, blocks):
                remaining[i] = remaining[i] - change[:, span(i - k - 1)]
        solved_ref[span(k), :] = mxu(inv_ref[span(k), :], own_rows)
        solved_parts.append(mxu(remaining[k], inv_ref[span(k), :]))

    def schur(piece, pairs):
        for t, (i, j) in enumerate(pairs):
            if j == 0:
                rows = mxu_tn(full_ref[:, span(i)], solved_ref[:, : (i + 1) * BLOCK])
            schur_ref[span(t), :] = rows[:, span(j)]

    def combine(s, work, land, semaphore):
        return pltpu.make_async_remote_copy(
            src_ref=work.at[s],
            dst_ref=land.at[s],
            send_sem=group_send.at[semaphore, s],
            recv_sem=group_recv.at[semaphore, s],
            device_id={"group": partners[s]},
            device_id_type=MESH,
        )

    schur(root_lead, root_lead_pairs)
    fill(schur_ref, len(root_lead_pairs) * BLOCK, None)
    work_lead[0] = own_lead - schur_ref[root_lead.slab_at(), :]
    combine(0, work_lead, land_lead, 0).start()
    schur(root_rest, root_rest_pairs)
    fill(schur_ref, root_base, mxu(jnp.concatenate(solved_parts, axis=1), full_ref[...]))
    work_rest[0] = own_rest - schur_ref[root_rest.slab_at(), :]
    combine(0, work_rest, land_rest, 1).start()
    for s in range(steps):
        for work, land, semaphore, piece in (
            (work_lead, land_lead, 0, root_lead),
            (work_rest, land_rest, 1, root_rest),
        ):
            combine(s, work, land, semaphore).wait()
            value = work[s] + land[s]
            if s + 1 < steps:
                work[s + 1] = value
                combine(s + 1, work, land, semaphore).start()
            else:
                piece.start_gather(value)
    advance(root_lead, 3)
    for k in reversed(range(blocks - 1)):
        later = slice((k + 1) * BLOCK, knots)
        row = row_ref[span(k), later]
        solved_ref[span(k), :] = solved_ref[span(k), :] - mxu(row, solved_ref[later, :])
        solved_parts[k] = solved_parts[k] - mxu_nt(
            jnp.concatenate(solved_parts[k + 1 :], axis=1), row
        )
    solved_rhs = jnp.concatenate(solved_parts, axis=1)
    advance(root_rest, 3)
    root_lead.finish()
    place_upper(inverse_ref, root_lead.total, root_prior_ref, root_lead_pairs)

    def root_arrive():
        root_rest.finish()
        place_upper(inverse_ref, root_rest.total, root_prior_ref, root_rest_pairs)

    tails = factor_tails(inverse_ref, row_ref, inv_ref, root_part, root_arrive)

    def forward(k):
        value = vector_ref[:, span(k)]
        found_ref[:, span(k)] = mxu(value, inv_ref[span(k), :])
        if k + 1 < root_blocks:
            later = slice((k + 1) * BLOCK, roots)
            vector_ref[:, later] = vector_ref[:, later] - mxu(value, row_ref[span(k), later])

    def with_forward(k, tail):
        if k == root_part - 1:
            tail()
            vector_ref[...] = unpack_row(root_rest.total, root_base, roots)
            for i in range(root_part):
                forward(i)
            return
        if tail is not None:
            tail()
        if k >= root_part:
            forward(k)

    each_block(
        inverse_ref, inv_ref, {},
        {k: functools.partial(with_forward, k, tails.get(k)) for k in range(root_blocks)},
    )
    weight_parts = [found_ref[:, span(k)] for k in range(root_blocks)]
    for k in reversed(range(root_blocks - 1)):
        weight_parts[k] = weight_parts[k] - mxu_nt(
            jnp.concatenate(weight_parts[k + 1 :], axis=1), row_ref[span(k), (k + 1) * BLOCK : roots]
        )
    weights = jnp.concatenate(weight_parts, axis=1)
    middle = solved_rhs - mxu_nt(weights, solved_ref[...])
    root_out[...] = weights[0:1, :]
    slab = mid_out.shape[1]
    turned = pltpu.roll(middle, (knots - me * slab) % knots, 1)
    mid_out[...] = turned[0:1, :slab]
    mid_rows = [jnp.broadcast_to(middle[0:1, span(j)], (BLOCK, BLOCK)) for j in range(blocks)]
    root_rows = [jnp.broadcast_to(weights[0:1, span(j)], (BLOCK, BLOCK)) for j in range(root_blocks)]

    for c in range(slots // BLOCK):
        at = span(c)
        total = jnp.zeros((BLOCK, BLOCK), jnp.float32)
        for j in range(blocks):
            total = total + basis_mid[at, span(j)] * mid_rows[j]
        for j in range(root_blocks):
            total = total + basis_root[at, span(j)] * root_rows[j]
        leaf_out[c : c + 1, :] = jnp.sum(total.T, axis=0, keepdims=True)


def round_up(value, unit):
    return (value + unit - 1) // unit * unit


def whole(observed, noise, mid_basis, root_basis, mid_prior, root_prior, leaf_count):
    slots, knots = mid_basis.shape
    roots = root_basis.shape[1]
    regions = lax.axis_size("region")
    members = lax.axis_size("group")
    steps = members.bit_length() - 1
    bits = regions.bit_length() - 1
    halving = tuple((bit, 1) for bit in range(bits))
    paired = ((0, 1), (1, bits - 1))
    orders = (paired, paired, halving, halving, paired, paired)
    unit = PANEL * regions
    blocks, root_blocks = knots // BLOCK, roots // BLOCK
    part, root_part = blocks // 2, root_blocks // 2
    sizes = [
        len(block_pairs(0, part)) * BLOCK,
        len(block_pairs(part, blocks)) * BLOCK,
        root_part * knots,
        (root_blocks - root_part) * knots + blocks,
        len(block_pairs(0, root_part)) * BLOCK,
        len(block_pairs(root_part, root_blocks)) * BLOCK + root_blocks,
    ]
    sizes = [round_up(size, unit) for size in sizes]

    def vmem(*shape):
        return pltpu.VMEM(shape, jnp.float32)

    def half(*shape):
        return pltpu.VMEM(shape, jnp.bfloat16)

    scratch = []
    for rows, order in zip(sizes, orders):
        counts = [1 << width for _, width in order]
        cuts = [rows]
        for count in counts:
            cuts.append(cuts[-1] // count)
        scratch.append(vmem(rows, BLOCK))
        scratch += [vmem(cut, BLOCK) for cut in cuts[:-1]]
        scratch += [vmem(count - 1, cut, BLOCK) for count, cut in zip(counts, cuts[1:])]
    scratch += [
        vmem(slots, knots),
        vmem(slots, roots),
        vmem(slots, BLOCK),
        vmem(slots, BLOCK),
        vmem(slots // BLOCK, BLOCK),
        vmem(slots // BLOCK, BLOCK),
        half(slots, knots),
        half(slots, knots),
        half(slots, roots),
        half(slots, roots),
        half(knots, slots),
        half(knots, slots),
        half(roots, slots),
        half(roots, slots),
        vmem(knots, knots),
        vmem(max(knots, roots), BLOCK),
        vmem(max(knots, roots), max(knots, roots)),
        vmem(knots, roots),
        vmem(knots, roots),
        vmem(max(sizes[4:]), BLOCK),
        vmem(PANEL, roots),
        vmem(PANEL, roots),
        vmem(steps, sizes[4] // regions, BLOCK),
        vmem(steps, sizes[4] // regions, BLOCK),
        vmem(steps, sizes[5] // regions, BLOCK),
        vmem(steps, sizes[5] // regions, BLOCK),
        pltpu.SemaphoreType.DMA((2, LOADS)),
        pltpu.SemaphoreType.DMA((2 * PIECES, bits, regions - 1)),
        pltpu.SemaphoreType.DMA((2 * PIECES, bits, regions - 1)),
        pltpu.SemaphoreType.DMA((2, steps)),
        pltpu.SemaphoreType.DMA((2, steps)),
    ]
    near = pl.BlockSpec(memory_space=pltpu.VMEM)
    far = pl.BlockSpec(memory_space=pl.ANY)
    return pl.pallas_call(
        functools.partial(whole_kernel, orders, members),
        out_shape=(
            jax.ShapeDtypeStruct((1, roots), jnp.float32),
            jax.ShapeDtypeStruct((1, knots // regions), jnp.float32),
            jax.ShapeDtypeStruct((slots // BLOCK, BLOCK), jnp.float32),
        ),
        in_specs=[near, near, far, far, near, near, near],
        out_specs=(near, near, near),
        scratch_shapes=scratch,
        compiler_params=pltpu.CompilerParams(
            collective_id=0, has_side_effects=True, vmem_limit_bytes=56 * 1024 * 1024
        ),
        name="posterior",
    )(
        observed.reshape(slots // BLOCK, BLOCK),
        noise.reshape(slots // BLOCK, BLOCK),
        mid_basis,
        root_basis,
        mid_prior,
        root_prior[None, :],
        leaf_count,
    )


def publish_kernel(*refs):
    for source, target in zip(refs[:3], refs[3:]):
        target[...] = source[...]


def on_device(observed, noise_precision, mid_basis, root_basis, mid_prior, root_prior, leaf_count):
    results = whole(
        observed, noise_precision, mid_basis, root_basis, mid_prior, root_prior, leaf_count
    )
    root_means, middle, leaf = pl.pallas_call(
        publish_kernel,
        out_shape=tuple(jax.ShapeDtypeStruct(x.shape, x.dtype) for x in results),
        name="publish",
    )(*results)
    return (root_means[0], middle, leaf.reshape(-1))


def solution(mesh):
    return jax.shard_map(
        on_device,
        mesh=mesh,
        in_specs=(
            P(("group", "region")),
            P(("group", "region")),
            P(("group", "region"), None),
            P(("group", "region"), None),
            P("group", None),
            P(),
            P("group", "region"),
        ),
        out_specs=(P(), P("group", "region"), P(("group", "region"))),
        check_vma=False,
    )
```
